32 devices in a mesh: frame: 2 (over x), depth: 4 (over z), row: 4 (over y, core).
Axes of the slice: x: 2, y: 2, z: 4, core: 2. Of those that a mesh axis runs over, the one named last changes fastest.
Arguments:
- volume: bfloat16 [4, 2, 8, 18432], P('depth', 'frame', 'row'), may hold values from -6 to 6
- point_spread: bfloat16 [4, 576, 25, 144], P('depth', 'frame', None, 'row'), may hold values from -0.046875 to 0.046875
- region_map: int32 [8, 128], replicated, may hold values from 0 to 3
- measured: bfloat16 [2, 8, 18432], P('frame', 'row', 'depth'), may hold values from -6 to 6
- pixel_weight: int32 [2, 8, 18432], P('frame', 'row', 'depth'), may hold values 0 or 1
Outputs:
- camera: float32 [2, 8, 18432], P('frame', 'row', 'depth')
- residual: float32 [2, 8, 18432], P('frame', 'row', 'depth')
The draws below stay inside these ranges and needn't reach their ends.
Inputs may be any that keep to these rules, and one draw needn't show every extreme that they name: `region_map`: the block that serves each lenslet.
All inputs are finite; a program needn't handle non-finite values. No bound on the sum of `pixel_weight` on one device may be relied on, other than what follows from the above.
Results may differ from the reference program's by a relative error of at most 0.0003.
Values may be sent and summed in bfloat16 or wider, within the bound.
A program may use at most 64 MiB of HBM per device.

```python
import jax
import jax.numpy as jnp
from jax import lax

PHASES = 144
BLOCKS = 4
TAP_SIDE = 5
LCOLS = 128
LROWS = 8
FRAMES = 2
DEPTHS = 4


def plant(array, key, smallest, largest):
    index_at = [jax.random.randint(jax.random.fold_in(key, axis), (), 0, length) for axis, length in enumerate(array.shape)]
    longest = array.shape.index(max(array.shape))
    beside = index_at[:longest] + [(index_at[longest] + 1) % array.shape[longest]] + index_at[longest + 1:]
    return array.at[tuple(index_at)].set(smallest).at[tuple(beside)].set(largest)


def shard_levels(stream_key, extent, shards, least, largest):
    loudness = 1.0
    for axis_at, shards_of in shards:
        steps = jax.random.uniform(jax.random.fold_in(jax.random.fold_in(stream_key, 6), axis_at), (shards_of,), jnp.float32, least / len(shards), largest / len(shards))
        loudness = loudness * jnp.repeat(jnp.exp(steps), extent[axis_at] // shards_of).reshape((-1,) + (1,) * (len(extent) - 1 - axis_at))
    return loudness


def gaussian(stream_key, shape, width, reach, cuts=(), kind=jnp.bfloat16):
    result = width * jax.random.normal(stream_key, shape, jnp.float32)
    if cuts:
        result = result * shard_levels(stream_key, shape, cuts, -0.22, 0.18)
    return jnp.clip(result, -reach, reach).astype(kind)


def setup_inputs(seed: int = 0) -> dict:
    streams_of = jax.random.split(jax.random.key(seed), 6)
    return {
        "volume": gaussian(streams_of[0], (DEPTHS, FRAMES, LROWS, LCOLS * PHASES), 1.0, 6.0, ((0, 4), (1, 2), (2, 4))),
        "point_spread": gaussian(streams_of[1], (DEPTHS, BLOCKS * PHASES, TAP_SIDE * TAP_SIDE, PHASES), (TAP_SIDE * TAP_SIDE * PHASES * DEPTHS) ** -0.5, 0.046875, ((0, 4), (1, 2), (3, 4))),
        "region_map": plant(jax.random.randint(streams_of[2], (LROWS, LCOLS), 0, BLOCKS), jax.random.fold_in(streams_of[2], 1), 0, BLOCKS - 1).astype(jnp.int32),
        "measured": gaussian(streams_of[3], (FRAMES, LROWS, LCOLS * PHASES), 1.0, 6.0, ((0, 2), (1, 4), (2, 4))),
        "pixel_weight": plant((jax.random.randint(streams_of[4], (FRAMES, LROWS, LCOLS * PHASES), 0, 4) < 3).astype(jnp.int32), jax.random.fold_in(streams_of[4], 1), 0, 1),
    }


def reference(volume, point_spread, region_map, measured, pixel_weight):
    tap_reach = TAP_SIDE // 2
    block_ids = jnp.arange(BLOCKS, dtype=jnp.int32)
    onehot = (region_map[:, :, None] == block_ids[None, None, :]).astype(jnp.float32)
    spread_all = point_spread.astype(jnp.float32)
    volume_split = volume.reshape(DEPTHS, FRAMES, LROWS, LCOLS, PHASES)

    def one_frame(planes):
        running = jnp.zeros((LROWS * LCOLS, PHASES), jnp.float32)
        for depth in range(DEPTHS):
            plane_now = planes[depth].astype(jnp.float32)
            expanded = (plane_now[:, :, None, :] * onehot[:, :, :, None]).reshape(LROWS, LCOLS, BLOCKS * PHASES)
            padded = jnp.pad(expanded, ((tap_reach, tap_reach), (tap_reach, tap_reach), (0, 0)))
            for tap_row in range(TAP_SIDE):
                for tap_col in range(TAP_SIDE):
                    first_row = 2 * tap_reach - tap_row
                    first_col = 2 * tap_reach - tap_col
                    shifted = padded[first_row:first_row + LROWS, first_col:first_col + LCOLS, :]
                    running = running + jnp.dot(shifted.reshape(LROWS * LCOLS, BLOCKS * PHASES),
                                                spread_all[depth, :, tap_row * TAP_SIDE + tap_col, :],
                                                precision=lax.Precision.HIGHEST)
        return running.reshape(LROWS, LCOLS * PHASES)

    camera = lax.map(one_frame, jnp.swapaxes(volume_split, 0, 1))
    residual = pixel_weight.astype(jnp.float32) * (camera - measured.astype(jnp.float32))
    return (camera, residual)
```

```python
import functools
import math

import jax
import jax.numpy as jnp
from jax import lax
from jax.experimental import pallas as pl
from jax.experimental.pallas import tpu as pltpu
from jax.sharding import PartitionSpec as P

PHASES = 144
BLOCKS = 4
TAP_SIDE = 5


def build_taps(planes, region_rows):
    tap_reach = TAP_SIDE // 2
    frames, row_count, merged = planes.shape
    col_count = merged // PHASES
    split_planes = planes.reshape(frames, row_count, col_count, PHASES)
    block_ids = jnp.arange(BLOCKS, dtype=jnp.int32)
    onehot = (region_rows[:, :, None] == block_ids[None, None, :]).astype(jnp.bfloat16)
    expanded = (split_planes[:, :, :, None, :] * onehot[None, :, :, :, None]).reshape(
        frames, row_count, col_count, BLOCKS * PHASES
    )
    return jnp.pad(expanded, ((0, 0), (0, 0), (tap_reach, tap_reach), (0, 0)))


def project(padded, spread_local, out_rows):
    tap_reach = TAP_SIDE // 2
    frames, ext_rows, ext_cols, _ = padded.shape
    col_count = ext_cols - 2 * tap_reach
    out_width = spread_local.shape[2]
    zero_start = jnp.zeros((frames * out_rows * col_count, out_width), jnp.float32)
    running = zero_start
    spread_slab = lax.all_gather(spread_local, "frame", axis=0, tiled=True)
    piece_rows = spread_slab.shape[0]
    flat_cols = padded.reshape(frames * ext_rows * ext_cols, piece_rows)
    for tap_row in range(TAP_SIDE):
        row_taps = spread_slab[:, tap_row * TAP_SIDE : (tap_row + 1) * TAP_SIDE, :].reshape(
            piece_rows, TAP_SIDE * out_width
        )
        product = jnp.dot(flat_cols, row_taps, preferred_element_type=jnp.float32)
        product = product.reshape(frames, ext_rows, ext_cols, TAP_SIDE, out_width)
        first_row = 2 * tap_reach - tap_row
        for tap_col in range(TAP_SIDE):
            first_col = 2 * tap_reach - tap_col
            shifted = product[
                :, first_row : first_row + out_rows, first_col : first_col + col_count, tap_col, :
            ]
            running = running + shifted.reshape(frames * out_rows * col_count, out_width)
    partial_value = running.reshape(frames, out_rows, col_count * out_width)
    return lax.psum_scatter(partial_value, "depth", scatter_dimension=2, tiled=True)


def plain_body(volume, point_spread, region_map, measured, pixel_weight):
    tap_reach = TAP_SIDE // 2
    planes = volume[0]
    row_count = planes.shape[1]
    region_padded = jnp.pad(region_map, ((tap_reach, tap_reach), (0, 0)), constant_values=-1)
    all_rows = lax.all_gather(planes, "row", axis=1, tiled=True)
    extended = jnp.pad(all_rows, ((0, 0), (tap_reach, tap_reach), (0, 0)))
    padded = build_taps(extended, region_padded)
    piece_width = point_spread.shape[3]
    partial_value = project(padded, point_spread[0], all_rows.shape[1])
    frames, total_rows, merged = partial_value.shape
    split_partial = partial_value.reshape(frames, total_rows, merged // piece_width, piece_width)
    returned = lax.all_to_all(split_partial, "row", split_axis=1, concat_axis=3, tiled=True)
    camera = returned.reshape(frames, row_count, returned.shape[2] * returned.shape[3])
    residual = pixel_weight.astype(jnp.float32) * (camera - measured.astype(jnp.float32))
    return (camera, residual)


def round_up(value, step):
    return (value + step - 1) // step * step


def remote(src, dst, send_sem, recv_sem, device):
    return pltpu.make_async_remote_copy(
        src_ref=src, dst_ref=dst, send_sem=send_sem, recv_sem=recv_sem,
        device_id=device, device_id_type=pl.DeviceIdType.MESH,
    )


def lanes_from_rows(raw, wide, pieces, vin):
    rows_here, phases, cols = vin.shape
    group = math.lcm(phases, 128) // phases
    span = group * phases
    groups = cols // group
    wide[:, span:] = jnp.zeros((wide.shape[0], wide.shape[1] - span), jnp.float32)
    for at in range(groups):
        strip = raw[:, at * span:(at + 1) * span].astype(jnp.float32)
        for row in range(rows_here):
            wide[row * groups + at:row * groups + at + 1, :span] = strip[row:row + 1]
    for member in range(group):
        for half in range(pieces.shape[0]):
            first = member * phases + half * 128
            pieces[half, pl.ds(member, rows_here * groups, stride=group), :] = wide[:, first:first + 128]
    for row in range(rows_here):
        for half in range(pieces.shape[0]):
            count = min(128, phases - half * 128)
            turned = pieces[half, row * cols:(row + 1) * cols, :].T
            vin[row, half * 128:half * 128 + count, :] = turned[:count].astype(jnp.bfloat16)


def kernel(frames, depths, row_shards, v_hbm, w_hbm, region_hbm, cam, region, region_sem, raw, wide, pieces, vin,
           in_sem, vol, wraw, wflat, xmask, part, xrecv, zsend,
           zrecv, yred, fin, w_sem, g_send, g_recv, x_send, x_recv, z_send, z_recv, y_send, y_recv):
    reach = TAP_SIDE // 2
    rows_here, phases, cols = vin.shape
    rows = rows_here * row_shards
    taps, width, depth_rows = w_hbm.shape
    blocks_here = depth_rows // phases
    stride = wflat.shape[0] // TAP_SIDE
    qpad = part.shape[3]
    col_share = cols // depths
    quads = rows // depths
    me_f, me_d, me_r = lax.axis_index("frame"), lax.axis_index("depth"), lax.axis_index("row")
    other_f = 1 - me_f
    core_r = me_r + 1 - 2 * lax.rem(me_r, 2)
    far_r = lax.rem(me_r + 2, row_shards)
    far_core_r = far_r + 1 - 2 * lax.rem(far_r, 2)


    x_dev = (other_f, me_d, me_r)
    core_dev = (me_f, me_d, core_r)
    far_dev = (me_f, me_d, far_r)
    diag_dev = (other_f, me_d, far_r)
    partners = [x_dev, diag_dev]
    partners += [(me_f, me_d, lax.rem(me_r + step, row_shards)) for step in range(1, row_shards)]
    partners += [(me_f, lax.rem(me_d + step, depths), me_r) for step in range(1, depths)]
    barrier = pltpu.get_barrier_semaphore()
    for device in partners:
        pl.semaphore_signal(barrier, inc=1, device_id=device, device_id_type=pl.DeviceIdType.MESH)
    v_copy = pltpu.make_async_copy(v_hbm, raw, in_sem.at[0])
    v_copy.start()
    w_copy = pltpu.make_async_copy(w_hbm, wraw, w_sem)
    w_copy.start()
    region_copy = pltpu.make_async_copy(region_hbm, region, region_sem)
    region_copy.start()
    v_copy.wait()
    lanes_from_rows(raw, wide, pieces, vin)
    pl.semaphore_wait(barrier, len(partners))

    def slot(frame, row):
        return vol.at[frame, pl.ds(row * rows_here, rows_here)]

    def gather(index, src, frame, row, device):
        return remote(src, slot(frame, row), g_send.at[index], g_recv.at[index], device)

    own_x = gather(0, vin, me_f, me_r, x_dev)
    own_far = gather(1, vin, me_f, me_r, far_dev)
    own_diag = gather(2, vin, me_f, me_r, diag_dev)
    own_core = gather(3, vin, me_f, me_r, core_dev)
    for copy in (own_x, own_far, own_diag, own_core):
        copy.start()
    slot(me_f, me_r)[...] = vin[...]

    w_copy.wait()
    region_copy.wait()
    for tap_col in range(TAP_SIDE):
        bands = [wraw[(TAP_SIDE - 1 - at) * TAP_SIDE + tap_col] for at in range(TAP_SIDE)]
        wflat[tap_col * stride:tap_col * stride + width, :] = jnp.concatenate(bands, axis=1)
    edge = jnp.zeros((reach * depth_rows, frames * cols), jnp.bfloat16)
    xmask[:reach * depth_rows, :] = edge
    xmask[(rows + reach) * depth_rows:, :] = edge

    own_x.wait_recv()
    fwd_x = gather(4, slot(other_f, me_r), other_f, me_r, core_dev)
    fwd_x.start()
    own_far.wait_recv()
    fwd_far = gather(5, slot(me_f, far_r), me_f, far_r, core_dev)
    fwd_far.start()
    own_diag.wait_recv()
    fwd_diag = gather(6, slot(other_f, far_r), other_f, far_r, core_dev)
    fwd_diag.start()
    for copy in (own_core, fwd_x, fwd_far, fwd_diag):
        copy.wait_recv()

    first_block = me_f * blocks_here
    for row in range(rows):
        for block in range(blocks_here):
            keep = (region[row:row + 1, :] == first_block + block).astype(jnp.float32).astype(jnp.bfloat16)
            top = (row + reach) * depth_rows + block * phases
            for frame in range(frames):
                xmask[top:top + phases, frame * cols:(frame + 1) * cols] = vol[frame, row] * keep

    lane = lax.broadcasted_iota(jnp.int32, (qpad, cols), 1)
    order = sorted(range(1, depths), key=lambda step: abs(step - depths // 2))
    x_copies, z_copies = {}, {}

    def frame_copy(quad, step):
        share = lax.rem(me_d + step, depths)
        return remote(part.at[other_f, quad, share], xrecv.at[quad, share], x_send.at[quad, step],
                      x_recv.at[quad, step], x_dev)

    for quad in range(quads):
        sums = [[None] * frames for _ in range(depths)]
        for at in range(depths):
            row = quad * depths + at
            slab = xmask[row * depth_rows:(row + TAP_SIDE) * depth_rows, :]
            product = jnp.dot(wflat[...], slab, preferred_element_type=jnp.float32)
            for frame in range(frames):
                total = None
                for tap_col in range(TAP_SIDE):
                    shift = tap_col - reach
                    piece = product[tap_col * stride:tap_col * stride + qpad, frame * cols:(frame + 1) * cols]
                    if shift:
                        piece = pltpu.roll(piece, shift % cols, 1)
                        inside = lane >= shift if shift > 0 else lane < cols + shift
                        piece = jnp.where(inside, piece, 0.0)
                    total = piece if total is None else total + piece
                sums[at][frame] = total
        for frame in range(frames):
            for share in range(depths):
                packed = None
                for at in range(depths):
                    shift = (at - share) * col_share % cols
                    moved = pltpu.roll(sums[at][frame], shift, 1) if shift else sums[at][frame]
                    packed = moved if packed is None else jnp.where(lane >= at * col_share, moved, packed)
                part[frame, quad, share] = packed
        for step in order:
            x_copies[quad, step] = frame_copy(quad, step)
            x_copies[quad, step].start()

    for quad in range(quads):
        x_copies[quad, 0] = frame_copy(quad, 0)
        x_copies[quad, 0].start()
    for quad in range(quads):
        for step in order:
            to = lax.rem(me_d + step, depths)
            x_copies[quad, step].wait_recv()
            zsend[quad, to] = part[me_f, quad, to] + xrecv[quad, to]
            z_copies[quad, step] = remote(zsend.at[quad, to], zrecv.at[quad, step - 1], z_send.at[quad, step - 1],
                                          z_recv.at[quad, step - 1], (me_f, to, me_r))
            z_copies[quad, step].start()
    shares = row_shards // quads

    def row_copy(to):
        return remote(yred.at[to // shares], fin.at[me_r], y_send.at[to], y_recv.at[me_r], (me_f, me_d, to))

    for quad in range(quads):
        x_copies[quad, 0].wait_recv()
        total = part[me_f, quad, me_d] + xrecv[quad, me_d]
        for step in order:
            z_copies[quad, step].wait_recv()
            total = total + zrecv[quad, step - 1]
        yred[quad] = total
        for to in range(quad * shares, (quad + 1) * shares):
            @pl.when(to != me_r)
            def _():
                row_copy(to).start()
    fin[me_r] = yred[me_r // shares]
    for source in range(row_shards):
        @pl.when(source != me_r)
        def _():
            remote(yred.at[0], fin.at[source], y_send.at[source], y_recv.at[source],
                   (me_f, me_d, source)).wait_recv()
            row_copy(source).wait_send()
    lanes_here = rows_here * col_share
    back = lax.rem(cols - lax.rem(me_r, shares) * lanes_here, cols)
    turned = jnp.concatenate(
        [pltpu.roll(fin[source], back, 1).T[:lanes_here, :width] for source in range(row_shards)], axis=1
    )
    halves = pieces.shape[0]
    for half in range(halves):
        count = min(128, phases - half * 128)
        pieces[half, :lanes_here, :count] = turned[:, half * 128:half * 128 + count]
    group = math.lcm(phases, 128) // phases
    span = group * phases
    per_row = col_share // group
    members = []
    for member in range(group):
        for half in range(halves):
            count = min(128, phases - half * 128)
            members.append(pieces[half, pl.ds(member, rows_here * per_row, stride=group), :][:, :count])
    strips = jnp.concatenate(members, axis=1)
    for row in range(rows_here):
        for at in range(per_row):
            line = row * per_row + at
            cam[row:row + 1, at * span:(at + 1) * span] = strips[line:line + 1]
    for copy in (own_x, own_far, own_diag, own_core, fwd_x, fwd_far, fwd_diag, *x_copies.values(), *z_copies.values()):
        copy.wait_send()


def hand_over(camera_in, recorded, weight, camera_out, residual_out):
    camera_out[...] = camera_in[...]
    residual_out[...] = weight[...].astype(jnp.float32) * (camera_in[...] - recorded[...].astype(jnp.float32))


def fused_body(sizes, volume, point_spread, region_map, measured, pixel_weight):
    frames, depths, row_shards = sizes
    _, _, rows_here, merged = volume.shape
    cols = merged // PHASES
    _, depth_rows, taps, width = point_spread.shape
    rows = rows_here * row_shards
    quads = rows // depths
    qpad = width
    stride = round_up(width, 16)
    group = math.lcm(PHASES, 128) // PHASES
    span = group * PHASES
    image = (rows_here, cols // depths * PHASES)
    spread = point_spread.reshape(depth_rows, taps, width).transpose(1, 2, 0)
    vmem = pl.BlockSpec(memory_space=pltpu.VMEM)
    hbm = pl.BlockSpec(memory_space=pltpu.HBM)
    dma = pltpu.SemaphoreType.DMA
    camera = pl.pallas_call(
        functools.partial(kernel, frames, depths, row_shards),
        out_shape=jax.ShapeDtypeStruct(image, jnp.float32),
        in_specs=[hbm, hbm, hbm],
        out_specs=vmem,
        scratch_shapes=[
            pltpu.VMEM(region_map.shape, jnp.int32),
            dma,
            pltpu.VMEM((rows_here, merged), jnp.bfloat16),
            pltpu.VMEM((rows_here * cols // group, span + 128), jnp.float32),
            pltpu.VMEM((round_up(PHASES, 128) // 128, rows_here * cols, 128), jnp.float32),
            pltpu.VMEM((rows_here, PHASES, cols), jnp.bfloat16),
            dma((1,)),
            pltpu.VMEM((frames, rows, PHASES, cols), jnp.bfloat16),
            pltpu.VMEM((taps, width, depth_rows), jnp.bfloat16),
            pltpu.VMEM((TAP_SIDE * stride, TAP_SIDE * depth_rows), jnp.bfloat16),
            pltpu.VMEM(((rows + TAP_SIDE - 1) * depth_rows, frames * cols), jnp.bfloat16),
            pltpu.VMEM((frames, quads, depths, qpad, cols), jnp.float32),
            pltpu.VMEM((quads, depths, qpad, cols), jnp.float32),
            pltpu.VMEM((quads, depths, qpad, cols), jnp.float32),
            pltpu.VMEM((quads, depths - 1, qpad, cols), jnp.float32),
            pltpu.VMEM((quads, qpad, cols), jnp.float32),
            pltpu.VMEM((row_shards, qpad, cols), jnp.float32),
            dma, dma((7,)), dma((7,)), dma((quads, depths)), dma((quads, depths)),
            dma((quads, depths - 1)), dma((quads, depths - 1)),
            dma((row_shards,)), dma((row_shards,)),
        ],
        compiler_params=pltpu.CompilerParams(collective_id=0, has_side_effects=True, vmem_limit_bytes=24 << 20),
    )(*[pltpu.with_memory_space_constraint(each, pltpu.HBM) for each in (volume.reshape(rows_here, merged), spread, region_map)])
    camera, residual = pl.pallas_call(
        hand_over,
        out_shape=[jax.ShapeDtypeStruct(image, jnp.float32)] * 2,
        in_specs=[vmem] * 3,
        out_specs=[vmem, vmem],
        compiler_params=pltpu.CompilerParams(vmem_limit_bytes=4 << 20),
    )(camera, measured.reshape(image), pixel_weight.reshape(image))
    return (camera.reshape(measured.shape), residual.reshape(measured.shape))


def solution(mesh):
    in_specs = (
        P("depth", "frame", "row", None),
        P("depth", "frame", None, "row"),
        P(),
        P("frame", "row", "depth"),
        P("frame", "row", "depth"),
    )
    out_specs = (P("frame", "row", "depth"), P("frame", "row", "depth"))
    sizes = (mesh.shape["frame"], mesh.shape["depth"], mesh.shape["row"])

    def body(volume, *rest):
        rows = volume.shape[2] * sizes[2]
        blocks_fit = rest[0].shape[1] % PHASES == 0
        quads = rows // sizes[1] if rows % sizes[1] == 0 else 0
        packs = quads and sizes[2] % quads == 0 and (volume.shape[3] // PHASES) == 128
        if sizes[0] == 2 and sizes[2] == 4 and volume.shape[1] == 1 and blocks_fit and packs:
            return fused_body(sizes, volume, *rest)
        return plain_body(volume, *rest)

    return jax.shard_map(body, mesh=mesh, in_specs=in_specs, out_specs=out_specs, check_vma=False)
```

```python
import functools
import math

import jax
import jax.numpy as jnp
from jax import lax
from jax.experimental import pallas as pl
from jax.experimental.pallas import tpu as pltpu
from jax.sharding import PartitionSpec as P

PHASES = 144
BLOCKS = 4
TAP_SIDE = 5
CORES = 2
LIMIT = 32000.0


def build_taps(planes, region_rows):
    tap_reach = TAP_SIDE // 2
    frames, row_count, merged = planes.shape
    col_count = merged // PHASES
    split_planes = planes.reshape(frames, row_count, col_count, PHASES)
    block_ids = jnp.arange(BLOCKS, dtype=jnp.int32)
    onehot = (region_rows[:, :, None] == block_ids[None, None, :]).astype(jnp.bfloat16)
    expanded = (split_planes[:, :, :, None, :] * onehot[None, :, :, :, None]).reshape(
        frames, row_count, col_count, BLOCKS * PHASES
    )
    return jnp.pad(expanded, ((0, 0), (0, 0), (tap_reach, tap_reach), (0, 0)))


def project(padded, spread_local, out_rows):
    tap_reach = TAP_SIDE // 2
    frames, ext_rows, ext_cols, _ = padded.shape
    col_count = ext_cols - 2 * tap_reach
    out_width = spread_local.shape[2]
    zero_start = jnp.zeros((frames * out_rows * col_count, out_width), jnp.float32)
    running = zero_start
    spread_slab = lax.all_gather(spread_local, "frame", axis=0, tiled=True)
    piece_rows = spread_slab.shape[0]
    flat_cols = padded.reshape(frames * ext_rows * ext_cols, piece_rows)
    for tap_row in range(TAP_SIDE):
        row_taps = spread_slab[:, tap_row * TAP_SIDE : (tap_row + 1) * TAP_SIDE, :].reshape(
            piece_rows, TAP_SIDE * out_width
        )
        product = jnp.dot(flat_cols, row_taps, preferred_element_type=jnp.float32)
        product = product.reshape(frames, ext_rows, ext_cols, TAP_SIDE, out_width)
        first_row = 2 * tap_reach - tap_row
        for tap_col in range(TAP_SIDE):
            first_col = 2 * tap_reach - tap_col
            shifted = product[
                :, first_row : first_row + out_rows, first_col : first_col + col_count, tap_col, :
            ]
            running = running + shifted.reshape(frames * out_rows * col_count, out_width)
    partial_value = running.reshape(frames, out_rows, col_count * out_width)
    return lax.psum_scatter(partial_value, "depth", scatter_dimension=2, tiled=True)


def plain_body(volume, point_spread, region_map, measured, pixel_weight):
    tap_reach = TAP_SIDE // 2
    planes = volume[0]
    row_count = planes.shape[1]
    region_padded = jnp.pad(region_map, ((tap_reach, tap_reach), (0, 0)), constant_values=-1)
    all_rows = lax.all_gather(planes, "row", axis=1, tiled=True)
    extended = jnp.pad(all_rows, ((0, 0), (tap_reach, tap_reach), (0, 0)))
    padded = build_taps(extended, region_padded)
    piece_width = point_spread.shape[3]
    partial_value = project(padded, point_spread[0], all_rows.shape[1])
    frames, total_rows, merged = partial_value.shape
    split_partial = partial_value.reshape(frames, total_rows, merged // piece_width, piece_width)
    returned = lax.all_to_all(split_partial, "row", split_axis=1, concat_axis=3, tiled=True)
    camera = returned.reshape(frames, row_count, returned.shape[2] * returned.shape[3])
    residual = pixel_weight.astype(jnp.float32) * (camera - measured.astype(jnp.float32))
    return (camera, residual)


def round_up(value, step):
    return (value + step - 1) // step * step


def remote(src, dst, send_sem, recv_sem, device):
    return pltpu.make_async_remote_copy(
        src_ref=src, dst_ref=dst, send_sem=send_sem, recv_sem=recv_sem,
        device_id=device, device_id_type=pl.DeviceIdType.MESH,
    )


def lanes_from_rows(raw, wide, pieces, vin):
    rows_here, phases, cols = vin.shape
    group = math.lcm(phases, 128) // phases
    span = group * phases
    groups = cols // group
    wide[:, span:] = jnp.zeros((wide.shape[0], wide.shape[1] - span), jnp.float32)
    for at in range(groups):
        strip = raw[:, at * span:(at + 1) * span].astype(jnp.float32)
        for row in range(rows_here):
            wide[row * groups + at:row * groups + at + 1, :span] = strip[row:row + 1]
    for member in range(group):
        for half in range(pieces.shape[0]):
            first = member * phases + half * 128
            pieces[half, pl.ds(member, rows_here * groups, stride=group), :] = wide[:, first:first + 128]
    for row in range(rows_here):
        for half in range(pieces.shape[0]):
            count = min(128, phases - half * 128)
            turned = pieces[half, row * cols:(row + 1) * cols, :].T
            vin[row, half * 128:half * 128 + count, :] = turned[:count].astype(jnp.bfloat16)


def kernel(frames, depths, row_shards, v_hbm, w_hbm, region_hbm, cam, raw, wide, pieces, vin, region, vol, wraw,
           wflat, slab, outbox, inbox, local_sem, g_send, g_recv, p_send, p_recv, m_send, m_recv):
    reach = TAP_SIDE // 2
    rows_here, phases, cols = vin.shape
    rows = rows_here * row_shards
    cores, taps, width, depth_rows = wraw.shape
    chips = row_shards // cores
    blocks_here = depth_rows // phases
    stack = cores * width
    col_share = cols // depths
    main = stack // (8 * depths) * 8
    per = 8 // depths
    me_f, me_d, me_r = lax.axis_index("frame"), lax.axis_index("depth"), lax.axis_index("row")
    me_y, me_c = me_r // cores, lax.rem(me_r, cores)
    other_f, other_y = 1 - me_f, 1 - me_y
    same = 1 - lax.rem(me_f + me_c, 2)
    core_dev = (me_f, me_d, me_y * cores + 1 - me_c)

    barrier = pltpu.get_barrier_semaphore()

    def greet(device):
        pl.semaphore_signal(barrier, inc=1, device_id=device, device_id_type=pl.DeviceIdType.MESH)

    for chip in range(chips):
        greet((me_c, me_d, chip * cores + other_f))
    for step in range(depths):
        for frame in range(frames):
            for chip in range(chips):
                device = (lax.rem(me_f + frame, frames), lax.rem(me_d + step, depths),
                          lax.rem(me_y + chip, chips) * cores + me_f)
                if step or frame or chip:
                    greet(device)
                else:
                    pl.when(same == 0)(functools.partial(greet, device))

    v_copy = pltpu.make_async_copy(v_hbm, raw, local_sem.at[0])
    v_copy.start()
    w_copy = pltpu.make_async_copy(w_hbm, wraw.at[me_c], local_sem.at[1])
    w_copy.start()
    region_copy = pltpu.make_async_copy(region_hbm, region, local_sem.at[2])
    region_copy.start()
    for block in (0, 1, rows + reach):
        slab[block * depth_rows:(block + 1) * depth_rows, :cols] = jnp.zeros((depth_rows, cols), jnp.bfloat16)
    for block in (0, rows + reach - 1, rows + reach):
        slab[block * depth_rows:(block + 1) * depth_rows, cols:] = jnp.zeros((depth_rows, cols), jnp.bfloat16)
    v_copy.wait()
    lanes_from_rows(raw, wide, pieces, vin)
    pl.semaphore_wait(barrier, frames * depths * chips + chips - same)

    def gather(index, device):
        return remote(vin, vol.at[me_r], g_send.at[index], g_recv.at[me_r], device)

    target = lax.rem(me_y, chips) * cores + me_f
    other_target = other_y * cores + me_f
    volume_copies = [gather(0, (other_f, me_d, target)), gather(1, (me_f, me_d, other_target)),
                     gather(2, (other_f, me_d, other_target))]
    core_copy = gather(3, core_dev)
    for copy in volume_copies:
        copy.start()

    @pl.when(same == 0)
    def _():
        core_copy.start()

    @pl.when(same == 1)
    def _():
        vol[me_r] = vin[...]

    w_send = remote(w_hbm, wraw.at[me_c], p_send, p_recv, core_dev)
    w_send.start()
    w_copy.wait()
    region_copy.wait()
    w_send.wait_recv()
    for tap_col in range(TAP_SIDE):
        bands = []
        for at in range(TAP_SIDE):
            tap = (TAP_SIDE - 1 - at) * TAP_SIDE + tap_col
            bands.append(jnp.concatenate([wraw[core, tap].astype(jnp.float32) for core in range(cores)], axis=0))
        wflat[tap_col * stack:(tap_col + 1) * stack, :] = jnp.concatenate(bands, axis=1).astype(jnp.bfloat16)

    lane = lax.broadcasted_iota(jnp.int32, (1, cols), 1)
    lane8 = lax.broadcasted_iota(jnp.int32, (8, cols), 1) // col_share
    row8 = lax.broadcasted_iota(jnp.int32, (8, cols), 0) // per
    turn = lax.rem(lane8 - row8 + depths, depths)
    first_block = me_f * blocks_here

    def take(chip):
        for core in range(cores):
            source = chip * cores + core

            def arrive():
                remote(vin, vol.at[source], g_send.at[0], g_recv.at[source], core_dev).wait_recv()
            pl.when((same == 0) | (source != me_r))(arrive)
            for row in range(rows_here):
                at = source * rows_here + row
                for block in range(blocks_here):
                    keep = (region[pl.ds(at, 1), :] == first_block + block).astype(jnp.float32).astype(jnp.bfloat16)
                    kept = vol[source, row] * keep
                    for lag in range(2):
                        top = pl.multiple_of((at + reach - lag) * depth_rows + block * phases, 16)
                        slab[pl.ds(top, phases), lag * cols:(lag + 1) * cols] = kept

    def message(index, share, pair, device_d):
        return remote(outbox.at[index, share], inbox.at[me_y, me_f, me_d], m_send.at[index, share],
                      m_recv.at[me_y, me_f, me_d], (me_c, device_d, pair))

    def work(index, pair):
        start = pl.multiple_of(pair * (rows_here * depth_rows), 16)
        product = jnp.dot(wflat[...], slab[pl.ds(start, TAP_SIDE * depth_rows), :],
                          preferred_element_type=jnp.float32)
        mains, extras = [], []
        for row in range(rows_here):
            total = None
            for tap_col in range(TAP_SIDE):
                shift = tap_col - reach
                piece = product[tap_col * stack:(tap_col + 1) * stack, row * cols:(row + 1) * cols]
                if shift:
                    piece = pltpu.roll(piece, shift % cols, 1)
                    inside = lane >= shift if shift > 0 else lane < cols + shift
                    piece = jnp.where(inside, piece, 0.0)
                total = piece if total is None else total + piece
            mains.append([total[block * main:(block + 1) * main] for block in range(depths)])
            rest = total[depths * main:]
            moved = rest
            for step in range(1, depths):
                rolled = pltpu.roll(pltpu.roll(rest, step * col_share, 1), 8 - per * step, 0)
                moved = jnp.where(turn == step, rolled, moved)
            extras.append(moved)
        tiles = []
        peak_rows = []
        peak_extra = jnp.maximum(jnp.abs(extras[0]), jnp.abs(extras[1]))
        for share in range(depths):
            pair_tiles = []
            for row in range(rows_here):
                packed = None
                for block in range(depths):
                    shift = (block - share) * col_share % cols
                    moved = mains[row][block]
                    moved = pltpu.roll(moved, shift, 1) if shift else moved
                    packed = moved if packed is None else jnp.where(lane >= block * col_share, moved, packed)
                pair_tiles.append(packed)
            tiles.append(pair_tiles)
            peak = jnp.maximum(jnp.abs(pair_tiles[0]), jnp.abs(pair_tiles[1]))
            peak = jnp.max(peak, axis=0, keepdims=True)
            peak = jnp.maximum(peak, jnp.max(peak_extra[per * share:per * (share + 1)], axis=0, keepdims=True))
            peak_rows += [peak] * per
        code = jnp.ceil(8.0 * jnp.log2(jnp.maximum(jnp.concatenate(peak_rows, axis=0), 1e-32)))
        inverse = LIMIT / jnp.exp2(code * 0.125)
        code = code.astype(jnp.int32)

        def words(upper, lower, factor):
            upper = jnp.round(upper * factor).astype(jnp.int32)
            lower = jnp.round(lower * factor).astype(jnp.int32)
            return (upper << 16) + lower

        rest = words(extras[0], extras[1], inverse)
        for share in range(depths):
            line = share * per
            outbox[index, share, :main] = words(*tiles[share], inverse[line:line + 1])
            outbox[index, share, main:main + per] = rest[line:line + per]
            outbox[index, share, main + per:] = code[line:line + 1]
        own = same * (pair == me_r).astype(jnp.int32)
        for step in (2, 1, 3, 0):
            to = lax.rem(me_d + step, depths)
            copy = message(index, to, pair, to)
            if step:
                copy.start()
            else:
                pl.when(own == 0)(copy.start)

                @pl.when(own == 1)
                def _():
                    inbox[me_y, me_f, me_d] = outbox[index, me_d]

    take(me_y)
    pairs = [me_y * (row_shards - 1) + (1 - 2 * me_y) * index for index in range(row_shards)]
    work(0, pairs[0])
    take(other_y)
    for index in range(1, row_shards):
        work(index, pairs[index])

    halves = []
    for chip_step in range(chips):
        chip = chip_step
        total = [None] * rows_here
        for frame_step in range(frames):
            frame = lax.rem(me_f + frame_step, frames)
            for step in range(depths):
                depth = lax.rem(me_d + step, depths)

                def arrive():
                    remote(outbox.at[0, 0], inbox.at[chip, frame, depth], m_send.at[0, 0],
                           m_recv.at[chip, frame, depth], core_dev).wait_recv()
                if frame_step or step:
                    arrive()
                else:
                    pl.when((same == 0) | (chip != me_y))(arrive)
                block = inbox[chip, frame, depth]
                scale = jnp.exp2(block[main + per:].astype(jnp.float32) * 0.125) * (1.0 / LIMIT)
                lower = (block << 16) >> 16
                upper = (block - lower).astype(jnp.float32) * (scale * (1.0 / 65536.0))
                lower = lower.astype(jnp.float32) * scale
                total = [term if held is None else held + term for held, term in zip(total, (upper, lower))]
        extra_rows = []
        for block in range(depths):
            moved = []
            for row in range(rows_here):
                shift = (row - block) * col_share % cols
                moved.append(pltpu.roll(total[row], shift, 1) if shift else total[row])
            merged = jnp.where(lane < col_share, moved[0], moved[1])
            halves.append(merged[:main])
            extra_rows.append(merged[main:main + per])
        halves.append(jnp.concatenate(extra_rows, axis=0))
    lanes_here = rows_here * col_share
    turned = jnp.concatenate(halves, axis=0).T[:lanes_here]
    group = math.lcm(phases, 128) // phases
    span = group * phases
    per_row = col_share // group
    members = []
    for half in range(pieces.shape[0]):
        count = min(128, phases - half * 128)
        pieces[half, :lanes_here, :count] = turned[:, half * 128:half * 128 + count]
    for member in range(group):
        for half in range(pieces.shape[0]):
            count = min(128, phases - half * 128)
            members.append(pieces[half, pl.ds(member, rows_here * per_row, stride=group), :][:, :count])
    strips = jnp.concatenate(members, axis=1)
    for row in range(rows_here):
        for at in range(per_row):
            line = row * per_row + at
            cam[row:row + 1, at * span:(at + 1) * span] = strips[line:line + 1]
    for copy in volume_copies:
        copy.wait_send()
    w_send.wait_send()
    pl.when(same == 0)(core_copy.wait_send)
    for index, pair in enumerate(pairs):
        own = same * (pair == me_r).astype(jnp.int32)
        for step in range(depths):
            to = lax.rem(me_d + step, depths)
            copy = message(index, to, pair, to)
            if step:
                copy.wait_send()
            else:
                pl.when(own == 0)(copy.wait_send)


def hand_over(camera_in, recorded, weight, camera_out, residual_out):
    camera_out[...] = camera_in[...]
    residual_out[...] = weight[...].astype(jnp.float32) * (camera_in[...] - recorded[...].astype(jnp.float32))


def fused_body(sizes, volume, point_spread, region_map, measured, pixel_weight):
    frames, depths, row_shards = sizes
    _, _, rows_here, merged = volume.shape
    cols = merged // PHASES
    _, depth_rows, taps, width = point_spread.shape
    rows = rows_here * row_shards
    stack = CORES * width
    lines = stack // depths + 1
    group = math.lcm(PHASES, 128) // PHASES
    span = group * PHASES
    image = (rows_here, cols // depths * PHASES)
    spread = point_spread.reshape(depth_rows, taps, width).transpose(1, 2, 0)
    vmem = pl.BlockSpec(memory_space=pltpu.VMEM)
    hbm = pl.BlockSpec(memory_space=pltpu.HBM)
    dma = pltpu.SemaphoreType.DMA
    camera = pl.pallas_call(
        functools.partial(kernel, frames, depths, row_shards),
        out_shape=jax.ShapeDtypeStruct(image, jnp.float32),
        in_specs=[hbm, hbm, hbm],
        out_specs=vmem,
        scratch_shapes=[
            pltpu.VMEM((rows_here, merged), jnp.bfloat16),
            pltpu.VMEM((rows_here * cols // group, span + 128), jnp.float32),
            pltpu.VMEM((round_up(PHASES, 128) // 128, rows_here * cols, 128), jnp.float32),
            pltpu.VMEM((rows_here, PHASES, cols), jnp.bfloat16),
            pltpu.VMEM(region_map.shape, jnp.int32),
            pltpu.VMEM((row_shards, rows_here, PHASES, cols), jnp.bfloat16),
            pltpu.VMEM((CORES, taps, width, depth_rows), jnp.bfloat16),
            pltpu.VMEM((TAP_SIDE * stack, TAP_SIDE * depth_rows), jnp.bfloat16),
            pltpu.VMEM(((rows + TAP_SIDE - 2) * depth_rows, rows_here * cols), jnp.bfloat16),
            pltpu.VMEM((row_shards, depths, lines, cols), jnp.int32),
            pltpu.VMEM((row_shards // CORES, frames, depths, lines, cols), jnp.int32),
            dma((3,)), dma((4,)), dma((row_shards,)), dma, dma, dma((row_shards, depths)),
            dma((row_shards // CORES, frames, depths)),
        ],
        compiler_params=pltpu.CompilerParams(collective_id=0, has_side_effects=True, vmem_limit_bytes=24 << 20),
    )(*[pltpu.with_memory_space_constraint(each, pltpu.HBM) for each in (volume.reshape(rows_here, merged), spread, region_map)])
    camera, residual = pl.pallas_call(
        hand_over,
        out_shape=[jax.ShapeDtypeStruct(image, jnp.float32)] * 2,
        in_specs=[vmem] * 3,
        out_specs=[vmem, vmem],
        compiler_params=pltpu.CompilerParams(vmem_limit_bytes=4 << 20),
    )(camera, measured.reshape(image), pixel_weight.reshape(image))
    return (camera.reshape(measured.shape), residual.reshape(measured.shape))


def solution(mesh):
    in_specs = (
        P("depth", "frame", "row", None),
        P("depth", "frame", None, "row"),
        P(),
        P("frame", "row", "depth"),
        P("frame", "row", "depth"),
    )
    out_specs = (P("frame", "row", "depth"), P("frame", "row", "depth"))
    sizes = (mesh.shape["frame"], mesh.shape["depth"], mesh.shape["row"])

    def body(volume, *rest):
        blocks_fit = rest[0].shape[1] % PHASES == 0
        stack = CORES * rest[0].shape[3]
        packs = sizes[1] == 4 and stack % 8 == 0 and stack // 8 % sizes[1] == 1
        pairs = volume.shape[2] == 2 and (volume.shape[3] // PHASES) == 128
        if sizes[0] == 2 and sizes[2] == 2 * CORES and volume.shape[1] == 1 and blocks_fit and packs and pairs:
            return fused_body(sizes, volume, *rest)
        return plain_body(volume, *rest)

    return jax.shard_map(body, mesh=mesh, in_specs=in_specs, out_specs=out_specs, check_vma=False)
```

```python
import functools
import math

import jax
import jax.numpy as jnp
from jax import lax
from jax.experimental import pallas as pl
from jax.experimental.pallas import tpu as pltpu
from jax.sharding import PartitionSpec as P

PHASES = 144
BLOCKS = 4
TAP_SIDE = 5
CORES = 2
LIMIT = 32000.0


def build_taps(planes, region_rows):
    tap_reach = TAP_SIDE // 2
    frames, row_count, merged = planes.shape
    col_count = merged // PHASES
    split_planes = planes.reshape(frames, row_count, col_count, PHASES)
    block_ids = jnp.arange(BLOCKS, dtype=jnp.int32)
    onehot = (region_rows[:, :, None] == block_ids[None, None, :]).astype(jnp.bfloat16)
    expanded = (split_planes[:, :, :, None, :] * onehot[None, :, :, :, None]).reshape(
        frames, row_count, col_count, BLOCKS * PHASES
    )
    return jnp.pad(expanded, ((0, 0), (0, 0), (tap_reach, tap_reach), (0, 0)))


def project(padded, spread_local, out_rows):
    tap_reach = TAP_SIDE // 2
    frames, ext_rows, ext_cols, _ = padded.shape
    col_count = ext_cols - 2 * tap_reach
    out_width = spread_local.shape[2]
    zero_start = jnp.zeros((frames * out_rows * col_count, out_width), jnp.float32)
    running = zero_start
    spread_slab = lax.all_gather(spread_local, "frame", axis=0, tiled=True)
    piece_rows = spread_slab.shape[0]
    flat_cols = padded.reshape(frames * ext_rows * ext_cols, piece_rows)
    for tap_row in range(TAP_SIDE):
        row_taps = spread_slab[:, tap_row * TAP_SIDE : (tap_row + 1) * TAP_SIDE, :].reshape(
            piece_rows, TAP_SIDE * out_width
        )
        product = jnp.dot(flat_cols, row_taps, preferred_element_type=jnp.float32)
        product = product.reshape(frames, ext_rows, ext_cols, TAP_SIDE, out_width)
        first_row = 2 * tap_reach - tap_row
        for tap_col in range(TAP_SIDE):
            first_col = 2 * tap_reach - tap_col
            shifted = product[
                :, first_row : first_row + out_rows, first_col : first_col + col_count, tap_col, :
            ]
            running = running + shifted.reshape(frames * out_rows * col_count, out_width)
    partial_value = running.reshape(frames, out_rows, col_count * out_width)
    return lax.psum_scatter(partial_value, "depth", scatter_dimension=2, tiled=True)


def plain_body(volume, point_spread, region_map, measured, pixel_weight):
    tap_reach = TAP_SIDE // 2
    planes = volume[0]
    row_count = planes.shape[1]
    region_padded = jnp.pad(region_map, ((tap_reach, tap_reach), (0, 0)), constant_values=-1)
    all_rows = lax.all_gather(planes, "row", axis=1, tiled=True)
    extended = jnp.pad(all_rows, ((0, 0), (tap_reach, tap_reach), (0, 0)))
    padded = build_taps(extended, region_padded)
    piece_width = point_spread.shape[3]
    partial_value = project(padded, point_spread[0], all_rows.shape[1])
    frames, total_rows, merged = partial_value.shape
    split_partial = partial_value.reshape(frames, total_rows, merged // piece_width, piece_width)
    returned = lax.all_to_all(split_partial, "row", split_axis=1, concat_axis=3, tiled=True)
    camera = returned.reshape(frames, row_count, returned.shape[2] * returned.shape[3])
    residual = pixel_weight.astype(jnp.float32) * (camera - measured.astype(jnp.float32))
    return (camera, residual)


def round_up(value, step):
    return (value + step - 1) // step * step


def remote(src, dst, send_sem, recv_sem, device):
    return pltpu.make_async_remote_copy(
        src_ref=src, dst_ref=dst, send_sem=send_sem, recv_sem=recv_sem,
        device_id=device, device_id_type=pl.DeviceIdType.MESH,
    )


def lanes_from_rows(raw, wide, pieces, vin):
    rows_here, phases, cols = vin.shape
    group = math.lcm(phases, 128) // phases
    span = group * phases
    groups = cols // group
    wide[:, span:] = jnp.zeros((wide.shape[0], wide.shape[1] - span), jnp.float32)
    for at in range(groups):
        strip = raw[:, at * span:(at + 1) * span].astype(jnp.float32)
        for row in range(rows_here):
            wide[row * groups + at:row * groups + at + 1, :span] = strip[row:row + 1]
    for member in range(group):
        for half in range(pieces.shape[0]):
            first = member * phases + half * 128
            pieces[half, pl.ds(member, rows_here * groups, stride=group), :] = wide[:, first:first + 128]
    for row in range(rows_here):
        for half in range(pieces.shape[0]):
            count = min(128, phases - half * 128)
            turned = pieces[half, row * cols:(row + 1) * cols, :].T
            vin[row, half * 128:half * 128 + count, :] = turned[:count].astype(jnp.bfloat16)


def kernel(frames, depths, row_shards, v_hbm, w_hbm, region_hbm, cam, raw, wide, pieces, vin, region, vol, wraw,
           wflat, slab, products, outbox, inbox, local_sem, g_send, g_recv, p_send, p_recv, m_send, m_recv):
    reach = TAP_SIDE // 2
    rows_here, phases, cols = vin.shape
    rows = rows_here * row_shards
    cores, taps, width, depth_rows = wraw.shape
    chips = row_shards // cores
    blocks_here = depth_rows // phases
    stack = cores * width
    col_share = cols // depths
    main = stack // (8 * depths) * 8
    per = 8 // depths
    me_f, me_d, me_r = lax.axis_index("frame"), lax.axis_index("depth"), lax.axis_index("row")
    me_y, me_c = me_r // cores, lax.rem(me_r, cores)
    other_f, other_y = 1 - me_f, 1 - me_y
    same = 1 - lax.rem(me_f + me_c, 2)
    core_dev = (me_f, me_d, me_y * cores + 1 - me_c)

    barrier = pltpu.get_barrier_semaphore()

    def greet(device):
        pl.semaphore_signal(barrier, inc=1, device_id=device, device_id_type=pl.DeviceIdType.MESH)

    for chip in range(chips):
        greet((me_c, me_d, chip * cores + other_f))
    for step in range(depths):
        for frame in range(frames):
            for chip in range(chips):
                device = (lax.rem(me_f + frame, frames), lax.rem(me_d + step, depths),
                          lax.rem(me_y + chip, chips) * cores + me_f)
                if step or frame or chip:
                    greet(device)
                else:
                    pl.when(same == 0)(functools.partial(greet, device))

    v_copy = pltpu.make_async_copy(v_hbm, raw, local_sem.at[0])
    v_copy.start()
    w_copy = pltpu.make_async_copy(w_hbm, wraw.at[me_c], local_sem.at[1])
    w_copy.start()
    region_copy = pltpu.make_async_copy(region_hbm, region, local_sem.at[2])
    region_copy.start()
    for block in (0, 1, rows + reach):
        slab[block * depth_rows:(block + 1) * depth_rows, :cols] = jnp.zeros((depth_rows, cols), jnp.bfloat16)
    for block in (0, rows + reach - 1, rows + reach):
        slab[block * depth_rows:(block + 1) * depth_rows, cols:] = jnp.zeros((depth_rows, cols), jnp.bfloat16)
    v_copy.wait()
    lanes_from_rows(raw, wide, pieces, vin)
    pl.semaphore_wait(barrier, frames * depths * chips + chips - same)

    def gather(index, device):
        return remote(vin, vol.at[me_r], g_send.at[index], g_recv.at[me_r], device)

    target = lax.rem(me_y, chips) * cores + me_f
    other_target = other_y * cores + me_f
    volume_copies = [gather(0, (other_f, me_d, target)), gather(1, (me_f, me_d, other_target)),
                     gather(2, (other_f, me_d, other_target))]
    core_copy = gather(3, core_dev)
    for copy in volume_copies:
        copy.start()

    @pl.when(same == 0)
    def _():
        core_copy.start()

    @pl.when(same == 1)
    def _():
        vol[me_r] = vin[...]

    w_copy.wait()
    w_send = remote(wraw.at[me_c], wraw.at[me_c], p_send, p_recv, core_dev)
    w_send.start()
    region_copy.wait()
    w_send.wait_recv()
    for tap_col in range(TAP_SIDE):
        bands = []
        for at in range(TAP_SIDE):
            tap = (TAP_SIDE - 1 - at) * TAP_SIDE + tap_col
            bands.append(jnp.concatenate([wraw[core, tap].astype(jnp.float32) for core in range(cores)], axis=0))
        wflat[tap_col * stack:(tap_col + 1) * stack, :] = jnp.concatenate(bands, axis=1).astype(jnp.bfloat16)

    lane = lax.broadcasted_iota(jnp.int32, (1, cols), 1)
    lane8 = lax.broadcasted_iota(jnp.int32, (8, cols), 1) // col_share
    row8 = lax.broadcasted_iota(jnp.int32, (8, cols), 0) // per
    turn = lax.rem(lane8 - row8 + depths, depths)
    first_block = me_f * blocks_here

    def take(chip):
        for core in range(cores):
            source = chip * cores + core

            def arrive():
                remote(vin, vol.at[source], g_send.at[0], g_recv.at[source], core_dev).wait_recv()
            pl.when((same == 0) | (source != me_r))(arrive)
            for row in range(rows_here):
                at = source * rows_here + row
                for block in range(blocks_here):
                    keep = (region[pl.ds(at, 1), :] == first_block + block).astype(jnp.float32).astype(jnp.bfloat16)
                    kept = vol[source, row] * keep
                    for lag in range(2):
                        top = pl.multiple_of((at + reach - lag) * depth_rows + block * phases, 16)
                        slab[pl.ds(top, phases), lag * cols:(lag + 1) * cols] = kept

    def message(index, share, pair, device_d):
        return remote(outbox.at[index, share], inbox.at[me_y, me_f, me_d], m_send.at[index, share],
                      m_recv.at[me_y, me_f, me_d], (me_c, device_d, pair))

    def multiply(index, pair):
        start = pl.multiple_of(pair * (rows_here * depth_rows), 16)
        cut = round_up(wflat.shape[0] // 2, 16)
        for low, high in ((0, cut), (cut, wflat.shape[0])):
            products[index % 2, low:high, :] = jnp.dot(
                wflat[low:high, :], slab[pl.ds(start, TAP_SIDE * depth_rows), :], preferred_element_type=jnp.float32)

    def pack(index):
        totals = []
        for row in range(rows_here):
            total = None
            for tap_col in range(TAP_SIDE):
                shift = tap_col - reach
                piece = products[index % 2, tap_col * stack:(tap_col + 1) * stack, row * cols:(row + 1) * cols]
                if shift:
                    piece = pltpu.roll(piece, shift % cols, 1)
                    inside = lane >= shift if shift > 0 else lane < cols + shift
                    piece = jnp.where(inside, piece, 0.0)
                total = piece if total is None else total + piece
            totals.append(total)
        peak = jnp.max(jnp.maximum(jnp.abs(totals[0]), jnp.abs(totals[1])), axis=0, keepdims=True)
        code = jnp.ceil(8.0 * jnp.log2(jnp.maximum(peak, 1e-32)))
        inverse = LIMIT / jnp.exp2(code * 0.125)
        upper, lower = [jnp.round(total * inverse).astype(jnp.int32) for total in totals]
        words = (upper << 16) + lower
        code = jnp.broadcast_to(code.astype(jnp.int32), turn.shape)
        tiles = [words[block * main:(block + 1) * main] for block in range(depths)]
        reach_blocks = depths // 2
        while reach_blocks:
            swap = reach_blocks * col_share
            for block in range(depths):
                if block & reach_blocks == 0:
                    first, second = tiles[block], tiles[block + reach_blocks]
                    stay = lane // col_share & reach_blocks == 0
                    tiles[block] = jnp.where(stay, first, pltpu.roll(second, swap, 1))
                    tiles[block + reach_blocks] = jnp.where(stay, pltpu.roll(first, cols - swap, 1), second)
            reach_blocks //= 2
        rest = words[depths * main:]
        moved, codes = rest, code
        for step in range(1, depths):
            rolled = pltpu.roll(pltpu.roll(rest, step * col_share, 1), 8 - per * step, 0)
            moved = jnp.where(turn == step, rolled, moved)
            codes = jnp.where(turn == step, pltpu.roll(code, step * col_share, 1), codes)
        for share in range(depths):
            line = share * per
            outbox[index, share, :main] = tiles[share]
            outbox[index, share, main:main + per] = moved[line:line + per]
            outbox[index, share, main + per:] = codes[line:line + 1]

    def each_message(index, pair, act, stay=None):
        for share in range(depths):
            copy = message(index, share, pair, share)
            if index == 2:
                act(copy)
                continue
            own = same * (pair == me_r).astype(jnp.int32) * (me_d == share).astype(jnp.int32)
            pl.when(own == 0)(functools.partial(act, copy))
            if stay is not None:
                pl.when(own == 1)(functools.partial(stay, index, share))

    def keep_own(index, share):
        inbox[me_y, me_f, me_d] = outbox[index, share]

    def send(index):
        each_message(index, pairs[index], lambda copy: copy.start(), keep_own)

    take(me_y)
    pairs = [me_y * (row_shards - 1)] + [index - me_y for index in range(1, row_shards)]
    multiply(0, pairs[0])
    pack(0)
    send(0)
    take(other_y)
    multiply(1, pairs[1])
    for index in range(1, row_shards):
        if index + 1 < row_shards:
            multiply(index + 1, pairs[index + 1])
        pack(index)
        send(index)
    halves = []
    for chip_step in range(chips):
        chip = chip_step
        total = [None] * rows_here
        for frame_step in range(frames):
            frame = lax.rem(me_f + frame_step, frames)
            for step in range(depths):
                depth = lax.rem(me_d + step, depths)

                def arrive():
                    remote(outbox.at[0, 0], inbox.at[chip, frame, depth], m_send.at[0, 0],
                           m_recv.at[chip, frame, depth], core_dev).wait_recv()
                if frame_step or step:
                    arrive()
                else:
                    pl.when((same == 0) | (chip != me_y))(arrive)
                block = inbox[chip, frame, depth]
                scale = jnp.exp2(block[main + per:].astype(jnp.float32) * 0.125) * (1.0 / LIMIT)
                lower = (block << 16) >> 16
                upper = (block - lower).astype(jnp.float32) * (scale * (1.0 / 65536.0))
                lower = lower.astype(jnp.float32) * scale
                total = [term if held is None else held + term for held, term in zip(total, (upper, lower))]
        extra_rows = []
        for block in range(depths):
            moved = []
            for row in range(rows_here):
                shift = (row - block) * col_share % cols
                moved.append(pltpu.roll(total[row], shift, 1) if shift else total[row])
            merged = jnp.where(lane < col_share, moved[0], moved[1])
            halves.append(merged[:main])
            extra_rows.append(merged[main:main + per])
        halves.append(jnp.concatenate(extra_rows, axis=0))
    lanes_here = rows_here * col_share
    turned = jnp.concatenate(halves, axis=0).T[:lanes_here]
    group = math.lcm(phases, 128) // phases
    span = group * phases
    per_row = col_share // group
    members = []
    for half in range(pieces.shape[0]):
        count = min(128, phases - half * 128)
        pieces[half, :lanes_here, :count] = turned[:, half * 128:half * 128 + count]
    for member in range(group):
        for half in range(pieces.shape[0]):
            count = min(128, phases - half * 128)
            members.append(pieces[half, pl.ds(member, rows_here * per_row, stride=group), :][:, :count])
    strips = jnp.concatenate(members, axis=1)
    for row in range(rows_here):
        for at in range(per_row):
            line = row * per_row + at
            cam[row:row + 1, at * span:(at + 1) * span] = strips[line:line + 1]
    for copy in volume_copies:
        copy.wait_send()
    w_send.wait_send()
    pl.when(same == 0)(core_copy.wait_send)
    for index, pair in enumerate(pairs):
        each_message(index, pair, lambda copy: copy.wait_send())


def hand_over(camera_in, recorded, weight, camera_out, residual_out):
    camera_out[...] = camera_in[...]
    residual_out[...] = weight[...].astype(jnp.float32) * (camera_in[...] - recorded[...].astype(jnp.float32))


def fused_body(sizes, volume, point_spread, region_map, measured, pixel_weight):
    frames, depths, row_shards = sizes
    _, _, rows_here, merged = volume.shape
    cols = merged // PHASES
    _, depth_rows, taps, width = point_spread.shape
    rows = rows_here * row_shards
    stack = CORES * width
    lines = stack // depths + 1
    group = math.lcm(PHASES, 128) // PHASES
    span = group * PHASES
    image = (rows_here, cols // depths * PHASES)
    spread = point_spread.reshape(depth_rows, taps, width).transpose(1, 2, 0)
    vmem = pl.BlockSpec(memory_space=pltpu.VMEM)
    hbm = pl.BlockSpec(memory_space=pltpu.HBM)
    dma = pltpu.SemaphoreType.DMA
    camera = pl.pallas_call(
        functools.partial(kernel, frames, depths, row_shards),
        out_shape=jax.ShapeDtypeStruct(image, jnp.float32),
        in_specs=[hbm, hbm, hbm],
        out_specs=vmem,
        scratch_shapes=[
            pltpu.VMEM((rows_here, merged), jnp.bfloat16),
            pltpu.VMEM((rows_here * cols // group, span + 128), jnp.float32),
            pltpu.VMEM((round_up(PHASES, 128) // 128, rows_here * cols, 128), jnp.float32),
            pltpu.VMEM((rows_here, PHASES, cols), jnp.bfloat16),
            pltpu.VMEM(region_map.shape, jnp.int32),
            pltpu.VMEM((row_shards, rows_here, PHASES, cols), jnp.bfloat16),
            pltpu.VMEM((CORES, taps, width, depth_rows), jnp.bfloat16),
            pltpu.VMEM((TAP_SIDE * stack, TAP_SIDE * depth_rows), jnp.bfloat16),
            pltpu.VMEM(((rows + TAP_SIDE - 2) * depth_rows, rows_here * cols), jnp.bfloat16),
            pltpu.VMEM((2, TAP_SIDE * stack, rows_here * cols), jnp.float32),
            pltpu.VMEM((row_shards, depths, lines, cols), jnp.int32),
            pltpu.VMEM((row_shards // CORES, frames, depths, lines, cols), jnp.int32),
            dma((3,)), dma((4,)), dma((row_shards,)), dma, dma, dma((row_shards, depths)),
            dma((row_shards // CORES, frames, depths)),
        ],
        compiler_params=pltpu.CompilerParams(collective_id=0, has_side_effects=True, vmem_limit_bytes=24 << 20),
    )(*[pltpu.with_memory_space_constraint(each, pltpu.HBM) for each in (volume.reshape(rows_here, merged), spread, region_map)])
    camera, residual = pl.pallas_call(
        hand_over,
        out_shape=[jax.ShapeDtypeStruct(image, jnp.float32)] * 2,
        in_specs=[vmem] * 3,
        out_specs=[vmem, vmem],
        compiler_params=pltpu.CompilerParams(vmem_limit_bytes=4 << 20),
    )(camera, measured.reshape(image), pixel_weight.reshape(image))
    return (camera.reshape(measured.shape), residual.reshape(measured.shape))


def solution(mesh):
    in_specs = (
        P("depth", "frame", "row", None),
        P("depth", "frame", None, "row"),
        P(),
        P("frame", "row", "depth"),
        P("frame", "row", "depth"),
    )
    out_specs = (P("frame", "row", "depth"), P("frame", "row", "depth"))
    sizes = (mesh.shape["frame"], mesh.shape["depth"], mesh.shape["row"])

    def body(volume, *rest):
        blocks_fit = rest[0].shape[1] % PHASES == 0
        stack = CORES * rest[0].shape[3]
        packs = sizes[1] == 4 and stack % 8 == 0 and stack // 8 % sizes[1] == 1
        pairs = volume.shape[2] == 2 and (volume.shape[3] // PHASES) == 128
        if sizes[0] == 2 and sizes[2] == 2 * CORES and volume.shape[1] == 1 and blocks_fit and packs and pairs:
            return fused_body(sizes, volume, *rest)
        return plain_body(volume, *rest)

    return jax.shard_map(body, mesh=mesh, in_specs=in_specs, out_specs=out_specs, check_vma=False)
```

```python
import functools
import math

import jax
import jax.numpy as jnp
from jax import lax
from jax.experimental import pallas as pl
from jax.experimental.pallas import tpu as pltpu
from jax.sharding import PartitionSpec as P

PHASES = 144
BLOCKS = 4
TAP_SIDE = 5
CORES = 2
LIMIT = 32000.0


def build_taps(planes, region_rows):
    tap_reach = TAP_SIDE // 2
    frames, row_count, merged = planes.shape
    col_count = merged // PHASES
    split_planes = planes.reshape(frames, row_count, col_count, PHASES)
    block_ids = jnp.arange(BLOCKS, dtype=jnp.int32)
    onehot = (region_rows[:, :, None] == block_ids[None, None, :]).astype(jnp.bfloat16)
    expanded = (split_planes[:, :, :, None, :] * onehot[None, :, :, :, None]).reshape(
        frames, row_count, col_count, BLOCKS * PHASES
    )
    return jnp.pad(expanded, ((0, 0), (0, 0), (tap_reach, tap_reach), (0, 0)))


def project(padded, spread_local, out_rows):
    tap_reach = TAP_SIDE // 2
    frames, ext_rows, ext_cols, _ = padded.shape
    col_count = ext_cols - 2 * tap_reach
    out_width = spread_local.shape[2]
    zero_start = jnp.zeros((frames * out_rows * col_count, out_width), jnp.float32)
    running = zero_start
    spread_slab = lax.all_gather(spread_local, "frame", axis=0, tiled=True)
    piece_rows = spread_slab.shape[0]
    flat_cols = padded.reshape(frames * ext_rows * ext_cols, piece_rows)
    for tap_row in range(TAP_SIDE):
        row_taps = spread_slab[:, tap_row * TAP_SIDE : (tap_row + 1) * TAP_SIDE, :].reshape(
            piece_rows, TAP_SIDE * out_width
        )
        product = jnp.dot(flat_cols, row_taps, preferred_element_type=jnp.float32)
        product = product.reshape(frames, ext_rows, ext_cols, TAP_SIDE, out_width)
        first_row = 2 * tap_reach - tap_row
        for tap_col in range(TAP_SIDE):
            first_col = 2 * tap_reach - tap_col
            shifted = product[
                :, first_row : first_row + out_rows, first_col : first_col + col_count, tap_col, :
            ]
            running = running + shifted.reshape(frames * out_rows * col_count, out_width)
    partial_value = running.reshape(frames, out_rows, col_count * out_width)
    return lax.psum_scatter(partial_value, "depth", scatter_dimension=2, tiled=True)


def plain_body(volume, point_spread, region_map, measured, pixel_weight):
    tap_reach = TAP_SIDE // 2
    planes = volume[0]
    row_count = planes.shape[1]
    region_padded = jnp.pad(region_map, ((tap_reach, tap_reach), (0, 0)), constant_values=-1)
    all_rows = lax.all_gather(planes, "row", axis=1, tiled=True)
    extended = jnp.pad(all_rows, ((0, 0), (tap_reach, tap_reach), (0, 0)))
    padded = build_taps(extended, region_padded)
    piece_width = point_spread.shape[3]
    partial_value = project(padded, point_spread[0], all_rows.shape[1])
    frames, total_rows, merged = partial_value.shape
    split_partial = partial_value.reshape(frames, total_rows, merged // piece_width, piece_width)
    returned = lax.all_to_all(split_partial, "row", split_axis=1, concat_axis=3, tiled=True)
    camera = returned.reshape(frames, row_count, returned.shape[2] * returned.shape[3])
    residual = pixel_weight.astype(jnp.float32) * (camera - measured.astype(jnp.float32))
    return (camera, residual)


def round_up(value, step):
    return (value + step - 1) // step * step


def remote(src, dst, send_sem, recv_sem, device):
    return pltpu.make_async_remote_copy(
        src_ref=src, dst_ref=dst, send_sem=send_sem, recv_sem=recv_sem,
        device_id=device, device_id_type=pl.DeviceIdType.MESH,
    )


def lanes_from_rows(raw, wide, pieces, vin):
    rows_here, phases, cols = vin.shape
    group = math.lcm(phases, 128) // phases
    span = group * phases
    groups = cols // group
    wide[:, span:] = jnp.zeros((wide.shape[0], wide.shape[1] - span), jnp.float32)
    for at in range(groups):
        strip = raw[:, at * span:(at + 1) * span].astype(jnp.float32)
        for row in range(rows_here):
            wide[row * groups + at:row * groups + at + 1, :span] = strip[row:row + 1]
    for member in range(group):
        for half in range(pieces.shape[0]):
            first = member * phases + half * 128
            pieces[half, pl.ds(member, rows_here * groups, stride=group), :] = wide[:, first:first + 128]
    for row in range(rows_here):
        for half in range(pieces.shape[0]):
            count = min(128, phases - half * 128)
            turned = pieces[half, row * cols:(row + 1) * cols, :].T
            vin[row, half * 128:half * 128 + count, :] = turned[:count].astype(jnp.bfloat16)


def kernel(frames, depths, row_shards, v_hbm, w_hbm, region_hbm, cam, raw, wide, pieces, vin, region, vol, wraw,
           wflat, slab, products, outbox, inbox, ready, local_sem, g_send, g_recv, p_send, p_recv, m_send, m_recv):
    reach = TAP_SIDE // 2
    rows_here, phases, cols = vin.shape
    rows = rows_here * row_shards
    cores, taps, width, depth_rows = wraw.shape
    chips = row_shards // cores
    blocks_here = depth_rows // phases
    stack = cores * width
    col_share = cols // depths
    main = stack // (8 * depths) * 8
    per = 8 // depths
    me_f, me_d, me_r = lax.axis_index("frame"), lax.axis_index("depth"), lax.axis_index("row")
    me_y, me_c = me_r // cores, lax.rem(me_r, cores)
    other_f, other_y = 1 - me_f, 1 - me_y
    same = 1 - lax.rem(me_f + me_c, 2)
    core_dev = (me_f, me_d, me_y * cores + 1 - me_c)

    barrier = pltpu.get_barrier_semaphore()

    def greet(device):
        pl.semaphore_signal(barrier, inc=1, device_id=device, device_id_type=pl.DeviceIdType.MESH)

    for chip in range(chips):
        for core in range(cores):
            to_chip, to_core = lax.rem(me_y + chip, chips), lax.rem(me_c + core, cores)
            device = (me_c, me_d, to_chip * cores + to_core)
            if chip or core:
                greet(device)
            else:
                pl.when(same == 0)(functools.partial(greet, device))
    pl.when(same == 0)(functools.partial(greet, core_dev))
    for step in range(1, depths):
        greet((me_f, lax.rem(me_d + step, depths), me_r))

    v_copy = pltpu.make_async_copy(v_hbm, raw, local_sem.at[0])
    v_copy.start()
    w_copy = pltpu.make_async_copy(w_hbm, wraw.at[me_c], local_sem.at[1])
    w_copy.start()
    region_copy = pltpu.make_async_copy(region_hbm, region, local_sem.at[2])
    region_copy.start()
    for block in (0, 1, rows + reach):
        slab[block * depth_rows:(block + 1) * depth_rows, :cols] = jnp.zeros((depth_rows, cols), jnp.bfloat16)
    for block in (0, rows + reach - 1, rows + reach):
        slab[block * depth_rows:(block + 1) * depth_rows, cols:] = jnp.zeros((depth_rows, cols), jnp.bfloat16)
    v_copy.wait()
    lanes_from_rows(raw, wide, pieces, vin)
    pl.semaphore_wait(barrier, frames * chips + depths - 1)

    def gather(index, device):
        return remote(vin, vol.at[me_r], g_send.at[index], g_recv.at[me_r], device)

    target = lax.rem(me_y, chips) * cores + me_f
    other_target = other_y * cores + me_f
    volume_copies = [gather(1, (me_f, me_d, other_target)),
                     gather(2, (other_f, me_d, other_target)),
                     gather(0, (other_f, me_d, target))]
    core_copy = gather(3, core_dev)
    for copy in volume_copies:
        copy.start()

    @pl.when(same == 0)
    def _():
        core_copy.start()

    @pl.when(same == 1)
    def _():
        vol[me_r] = vin[...]

    for frame in range(frames):
        for chip in range(chips):
            device = (lax.rem(me_f + frame, frames), me_d, lax.rem(me_y + chip, chips) * cores + me_f)
            if frame or chip:
                pl.semaphore_signal(ready, inc=1, device_id=device, device_id_type=pl.DeviceIdType.MESH)
            else:
                @pl.when(same == 0)
                def _():
                    pl.semaphore_signal(ready, inc=1, device_id=device, device_id_type=pl.DeviceIdType.MESH)
    w_copy.wait()
    w_send = remote(wraw.at[me_c], wraw.at[me_c], p_send, p_recv, core_dev)
    w_send.start()
    region_copy.wait()
    w_send.wait_recv()
    for tap_col in range(TAP_SIDE):
        bands = []
        for at in range(TAP_SIDE):
            tap = (TAP_SIDE - 1 - at) * TAP_SIDE + tap_col
            bands.append(jnp.concatenate([wraw[core, tap].astype(jnp.float32) for core in range(cores)], axis=0))
        wflat[tap_col * stack:(tap_col + 1) * stack, :] = jnp.concatenate(bands, axis=1).astype(jnp.bfloat16)

    lane = lax.broadcasted_iota(jnp.int32, (1, cols), 1)
    lane8 = lax.broadcasted_iota(jnp.int32, (8, cols), 1) // col_share
    row8 = lax.broadcasted_iota(jnp.int32, (8, cols), 0) // per
    turn = lax.rem(lane8 - row8 + depths, depths)
    first_block = me_f * blocks_here

    def take(chip):
        for core in range(cores):
            source = chip * cores + core

            def arrive():
                remote(vin, vol.at[source], g_send.at[0], g_recv.at[source], core_dev).wait_recv()
            pl.when((same == 0) | (source != me_r))(arrive)
            for row in range(rows_here):
                at = source * rows_here + row
                for block in range(blocks_here):
                    keep = (region[pl.ds(at, 1), :] == first_block + block).astype(jnp.float32).astype(jnp.bfloat16)
                    kept = vol[source, row] * keep
                    for lag in range(2):
                        top = pl.multiple_of((at + reach - lag) * depth_rows + block * phases, 16)
                        slab[pl.ds(top, phases), lag * cols:(lag + 1) * cols] = kept

    def message(index, share, pair, device_d):
        return remote(outbox.at[index, share], inbox.at[me_y, me_f, me_d], m_send.at[index, share],
                      m_recv.at[me_y, me_f, me_d], (me_c, device_d, pair))

    def multiply(index, pair):
        start = pl.multiple_of(pair * (rows_here * depth_rows), 16)
        cut = round_up(wflat.shape[0] // 2, 16)
        for low, high in ((0, cut), (cut, wflat.shape[0])):
            products[index % 2, low:high, :] = jnp.dot(
                wflat[low:high, :], slab[pl.ds(start, TAP_SIDE * depth_rows), :], preferred_element_type=jnp.float32)

    def pack(index):
        totals = []
        for row in range(rows_here):
            total = None
            for tap_col in range(TAP_SIDE):
                shift = tap_col - reach
                piece = products[index % 2, tap_col * stack:(tap_col + 1) * stack, row * cols:(row + 1) * cols]
                if shift:
                    piece = pltpu.roll(piece, shift % cols, 1)
                    inside = lane >= shift if shift > 0 else lane < cols + shift
                    piece = jnp.where(inside, piece, 0.0)
                total = piece if total is None else total + piece
            totals.append(total)
        peak = jnp.max(jnp.maximum(jnp.abs(totals[0]), jnp.abs(totals[1])), axis=0, keepdims=True)
        code = jnp.ceil(8.0 * jnp.log2(jnp.maximum(peak, 1e-32)))
        inverse = LIMIT / jnp.exp2(code * 0.125)
        upper, lower = [jnp.round(total * inverse).astype(jnp.int32) for total in totals]
        words = (upper << 16) + lower
        code = jnp.broadcast_to(code.astype(jnp.int32), turn.shape)
        tiles = [words[block * main:(block + 1) * main] for block in range(depths)]
        reach_blocks = depths // 2
        while reach_blocks:
            swap = reach_blocks * col_share
            for block in range(depths):
                if block & reach_blocks == 0:
                    first, second = tiles[block], tiles[block + reach_blocks]
                    stay = lane // col_share & reach_blocks == 0
                    tiles[block] = jnp.where(stay, first, pltpu.roll(second, swap, 1))
                    tiles[block + reach_blocks] = jnp.where(stay, pltpu.roll(first, cols - swap, 1), second)
            reach_blocks //= 2
        rest = words[depths * main:]
        moved, codes = rest, code
        for step in range(1, depths):
            rolled = pltpu.roll(pltpu.roll(rest, step * col_share, 1), 8 - per * step, 0)
            moved = jnp.where(turn == step, rolled, moved)
            codes = jnp.where(turn == step, pltpu.roll(code, step * col_share, 1), codes)
        for share in range(depths):
            line = share * per
            outbox[index, share, :main] = tiles[share]
            outbox[index, share, main:main + per] = moved[line:line + per]
            outbox[index, share, main + per:] = codes[line:line + 1]

    def each_message(index, pair, act, stay=None):
        for share in range(depths):
            copy = message(index, share, pair, share)
            if index == 2:
                act(copy)
                continue
            own = same * (pair == me_r).astype(jnp.int32) * (me_d == share).astype(jnp.int32)
            pl.when(own == 0)(functools.partial(act, copy))
            if stay is not None:
                pl.when(own == 1)(functools.partial(stay, index, share))

    def keep_own(index, share):
        inbox[me_y, me_f, me_d] = outbox[index, share]

    def send(index):
        each_message(index, pairs[index], lambda copy: copy.start(), keep_own)

    first = other_y + same * (me_y - other_y)
    take(first)
    pairs = [first * (row_shards - 1)] + [index - first for index in range(1, row_shards)]
    multiply(0, pairs[0])
    pack(0)
    pl.semaphore_wait(ready, row_shards - same)
    send(0)
    take(1 - first)
    multiply(1, pairs[1])
    for index in range(1, row_shards):
        if index + 1 < row_shards:
            multiply(index + 1, pairs[index + 1])
        pack(index)
        send(index)
    halves = []
    for chip_step in range(chips):
        chip = chip_step
        total = [None] * rows_here
        for frame_step in range(frames):
            frame = lax.rem(me_f + frame_step, frames)
            for step in range(depths):
                depth = lax.rem(me_d + step, depths)

                def arrive():
                    remote(outbox.at[0, 0], inbox.at[chip, frame, depth], m_send.at[0, 0],
                           m_recv.at[chip, frame, depth], core_dev).wait_recv()
                if frame_step or step:
                    arrive()
                else:
                    pl.when((same == 0) | (chip != me_y))(arrive)
                block = inbox[chip, frame, depth]
                scale = jnp.exp2(block[main + per:].astype(jnp.float32) * 0.125) * (1.0 / LIMIT)
                lower = (block << 16) >> 16
                upper = (block - lower).astype(jnp.float32) * (scale * (1.0 / 65536.0))
                lower = lower.astype(jnp.float32) * scale
                total = [term if held is None else held + term for held, term in zip(total, (upper, lower))]
        extra_rows = []
        for block in range(depths):
            moved = []
            for row in range(rows_here):
                shift = (row - block) * col_share % cols
                moved.append(pltpu.roll(total[row], shift, 1) if shift else total[row])
            merged = jnp.where(lane < col_share, moved[0], moved[1])
            halves.append(merged[:main])
            extra_rows.append(merged[main:main + per])
        halves.append(jnp.concatenate(extra_rows, axis=0))
    lanes_here = rows_here * col_share
    turned = jnp.concatenate(halves, axis=0).T[:lanes_here]
    group = math.lcm(phases, 128) // phases
    span = group * phases
    per_row = col_share // group
    members = []
    for half in range(pieces.shape[0]):
        count = min(128, phases - half * 128)
        pieces[half, :lanes_here, :count] = turned[:, half * 128:half * 128 + count]
    for member in range(group):
        for half in range(pieces.shape[0]):
            count = min(128, phases - half * 128)
            members.append(pieces[half, pl.ds(member, rows_here * per_row, stride=group), :][:, :count])
    strips = jnp.concatenate(members, axis=1)
    for row in range(rows_here):
        for at in range(per_row):
            line = row * per_row + at
            cam[row:row + 1, at * span:(at + 1) * span] = strips[line:line + 1]
    for copy in volume_copies:
        copy.wait_send()
    w_send.wait_send()
    pl.when(same == 0)(core_copy.wait_send)
    for index, pair in enumerate(pairs):
        each_message(index, pair, lambda copy: copy.wait_send())


def hand_over(camera_in, recorded, weight, camera_out, residual_out):
    camera_out[...] = camera_in[...]
    residual_out[...] = weight[...].astype(jnp.float32) * (camera_in[...] - recorded[...].astype(jnp.float32))


def fused_body(sizes, volume, point_spread, region_map, measured, pixel_weight):
    frames, depths, row_shards = sizes
    _, _, rows_here, merged = volume.shape
    cols = merged // PHASES
    _, depth_rows, taps, width = point_spread.shape
    rows = rows_here * row_shards
    stack = CORES * width
    lines = stack // depths + 1
    group = math.lcm(PHASES, 128) // PHASES
    span = group * PHASES
    image = (rows_here, cols // depths * PHASES)
    spread = point_spread.reshape(depth_rows, taps, width).transpose(1, 2, 0)
    vmem = pl.BlockSpec(memory_space=pltpu.VMEM)
    hbm = pl.BlockSpec(memory_space=pltpu.HBM)
    dma = pltpu.SemaphoreType.DMA
    camera = pl.pallas_call(
        functools.partial(kernel, frames, depths, row_shards),
        out_shape=jax.ShapeDtypeStruct(image, jnp.float32),
        in_specs=[hbm, hbm, hbm],
        out_specs=vmem,
        scratch_shapes=[
            pltpu.VMEM((rows_here, merged), jnp.bfloat16),
            pltpu.VMEM((rows_here * cols // group, span + 128), jnp.float32),
            pltpu.VMEM((round_up(PHASES, 128) // 128, rows_here * cols, 128), jnp.float32),
            pltpu.VMEM((rows_here, PHASES, cols), jnp.bfloat16),
            pltpu.VMEM(region_map.shape, jnp.int32),
            pltpu.VMEM((row_shards, rows_here, PHASES, cols), jnp.bfloat16),
            pltpu.VMEM((CORES, taps, width, depth_rows), jnp.bfloat16),
            pltpu.VMEM((TAP_SIDE * stack, TAP_SIDE * depth_rows), jnp.bfloat16),
            pltpu.VMEM(((rows + TAP_SIDE - 2) * depth_rows, rows_here * cols), jnp.bfloat16),
            pltpu.VMEM((2, TAP_SIDE * stack, rows_here * cols), jnp.float32),
            pltpu.VMEM((row_shards, depths, lines, cols), jnp.int32),
            pltpu.VMEM((row_shards // CORES, frames, depths, lines, cols), jnp.int32),
            pltpu.SemaphoreType.REGULAR, dma((3,)), dma((4,)), dma((row_shards,)), dma, dma, dma((row_shards, depths)),
            dma((row_shards // CORES, frames, depths)),
        ],
        compiler_params=pltpu.CompilerParams(collective_id=0, has_side_effects=True, vmem_limit_bytes=24 << 20),
    )(*[pltpu.with_memory_space_constraint(each, pltpu.HBM) for each in (volume.reshape(rows_here, merged), spread, region_map)])
    camera, residual = pl.pallas_call(
        hand_over,
        out_shape=[jax.ShapeDtypeStruct(image, jnp.float32)] * 2,
        in_specs=[vmem] * 3,
        out_specs=[vmem, vmem],
        compiler_params=pltpu.CompilerParams(vmem_limit_bytes=4 << 20),
    )(camera, measured.reshape(image), pixel_weight.reshape(image))
    return (camera.reshape(measured.shape), residual.reshape(measured.shape))


def solution(mesh):
    in_specs = (
        P("depth", "frame", "row", None),
        P("depth", "frame", None, "row"),
        P(),
        P("frame", "row", "depth"),
        P("frame", "row", "depth"),
    )
    out_specs = (P("frame", "row", "depth"), P("frame", "row", "depth"))
    sizes = (mesh.shape["frame"], mesh.shape["depth"], mesh.shape["row"])

    def body(volume, *rest):
        blocks_fit = rest[0].shape[1] % PHASES == 0
        stack = CORES * rest[0].shape[3]
        packs = sizes[1] == 4 and stack % 8 == 0 and stack // 8 % sizes[1] == 1
        pairs = volume.shape[2] == 2 and (volume.shape[3] // PHASES) == 128
        if sizes[0] == 2 and sizes[2] == 2 * CORES and volume.shape[1] == 1 and blocks_fit and packs and pairs:
            return fused_body(sizes, volume, *rest)
        return plain_body(volume, *rest)

    return jax.shard_map(body, mesh=mesh, in_specs=in_specs, out_specs=out_specs, check_vma=False)
```

```python
import functools
import math

import jax
import jax.numpy as jnp
from jax import lax
from jax.experimental import pallas as pl
from jax.experimental.pallas import tpu as pltpu
from jax.sharding import PartitionSpec as P

PHASES = 144
BLOCKS = 4
TAP_SIDE = 5
CORES = 2
LIMIT = 32000.0


def build_taps(planes, region_rows):
    tap_reach = TAP_SIDE // 2
    frames, row_count, merged = planes.shape
    col_count = merged // PHASES
    split_planes = planes.reshape(frames, row_count, col_count, PHASES)
    block_ids = jnp.arange(BLOCKS, dtype=jnp.int32)
    onehot = (region_rows[:, :, None] == block_ids[None, None, :]).astype(jnp.bfloat16)
    expanded = (split_planes[:, :, :, None, :] * onehot[None, :, :, :, None]).reshape(
        frames, row_count, col_count, BLOCKS * PHASES
    )
    return jnp.pad(expanded, ((0, 0), (0, 0), (tap_reach, tap_reach), (0, 0)))


def project(padded, spread_local, out_rows):
    tap_reach = TAP_SIDE // 2
    frames, ext_rows, ext_cols, _ = padded.shape
    col_count = ext_cols - 2 * tap_reach
    out_width = spread_local.shape[2]
    zero_start = jnp.zeros((frames * out_rows * col_count, out_width), jnp.float32)
    running = zero_start
    spread_slab = lax.all_gather(spread_local, "frame", axis=0, tiled=True)
    piece_rows = spread_slab.shape[0]
    flat_cols = padded.reshape(frames * ext_rows * ext_cols, piece_rows)
    for tap_row in range(TAP_SIDE):
        row_taps = spread_slab[:, tap_row * TAP_SIDE : (tap_row + 1) * TAP_SIDE, :].reshape(
            piece_rows, TAP_SIDE * out_width
        )
        product = jnp.dot(flat_cols, row_taps, preferred_element_type=jnp.float32)
        product = product.reshape(frames, ext_rows, ext_cols, TAP_SIDE, out_width)
        first_row = 2 * tap_reach - tap_row
        for tap_col in range(TAP_SIDE):
            first_col = 2 * tap_reach - tap_col
            shifted = product[
                :, first_row : first_row + out_rows, first_col : first_col + col_count, tap_col, :
            ]
            running = running + shifted.reshape(frames * out_rows * col_count, out_width)
    partial_value = running.reshape(frames, out_rows, col_count * out_width)
    return lax.psum_scatter(partial_value, "depth", scatter_dimension=2, tiled=True)


def plain_body(volume, point_spread, region_map, measured, pixel_weight):
    tap_reach = TAP_SIDE // 2
    planes = volume[0]
    row_count = planes.shape[1]
    region_padded = jnp.pad(region_map, ((tap_reach, tap_reach), (0, 0)), constant_values=-1)
    all_rows = lax.all_gather(planes, "row", axis=1, tiled=True)
    extended = jnp.pad(all_rows, ((0, 0), (tap_reach, tap_reach), (0, 0)))
    padded = build_taps(extended, region_padded)
    piece_width = point_spread.shape[3]
    partial_value = project(padded, point_spread[0], all_rows.shape[1])
    frames, total_rows, merged = partial_value.shape
    split_partial = partial_value.reshape(frames, total_rows, merged // piece_width, piece_width)
    returned = lax.all_to_all(split_partial, "row", split_axis=1, concat_axis=3, tiled=True)
    camera = returned.reshape(frames, row_count, returned.shape[2] * returned.shape[3])
    residual = pixel_weight.astype(jnp.float32) * (camera - measured.astype(jnp.float32))
    return (camera, residual)


def round_up(value, step):
    return (value + step - 1) // step * step


def remote(src, dst, send_sem, recv_sem, device):
    return pltpu.make_async_remote_copy(
        src_ref=src, dst_ref=dst, send_sem=send_sem, recv_sem=recv_sem,
        device_id=device, device_id_type=pl.DeviceIdType.MESH,
    )


def lanes_from_rows(raw, wide, pieces, vin):
    _, phases, cols = vin.shape
    rows_here = raw.shape[0]
    group = math.lcm(phases, 128) // phases
    span = group * phases
    groups = cols // group
    wide[:, span:] = jnp.zeros((wide.shape[0], wide.shape[1] - span), jnp.float32)
    for at in range(groups):
        strip = raw[:, at * span:(at + 1) * span].astype(jnp.float32)
        for row in range(rows_here):
            wide[row * groups + at:row * groups + at + 1, :span] = strip[row:row + 1]
    for member in range(group):
        for half in range(pieces.shape[0]):
            first = member * phases + half * 128
            pieces[half, pl.ds(member, rows_here * groups, stride=group), :] = wide[:, first:first + 128]
    side = cols // 2
    for part in range(2):
        for half in range(pieces.shape[0]):
            count = min(128, phases - half * 128)
            rows = [pieces[half, row * cols + part * side:row * cols + (part + 1) * side, :] for row in range(rows_here)]
            turned = jnp.concatenate(rows[::-1] if part else rows, axis=0).T
            vin[part, half * 128:half * 128 + count, :] = turned[:count].astype(jnp.bfloat16)


def kernel(frames, depths, row_shards, v_hbm, w_hbm, region_hbm, cam, raw, wide, pieces, vin, region, vol, wraw,
           wflat, slab, products, sums, outbox, inbox, ready, local_sem, g_send, g_recv, p_send, p_recv, m_send, m_recv):
    reach = TAP_SIDE // 2
    _, phases, cols = vin.shape
    rows_here = raw.shape[0]
    side = cols // 2
    rows = rows_here * row_shards
    cores, taps, width, depth_rows = wraw.shape
    chips = row_shards // cores
    blocks_here = depth_rows // phases
    stack = cores * width
    col_share = cols // depths
    main = stack // (8 * depths) * 8
    per = 8 // depths
    me_f, me_d, me_r = lax.axis_index("frame"), lax.axis_index("depth"), lax.axis_index("row")
    me_y, me_c = me_r // cores, lax.rem(me_r, cores)
    other_f, other_y = 1 - me_f, 1 - me_y
    same = 1 - lax.rem(me_f + me_c, 2)
    core_dev = (me_f, me_d, me_y * cores + 1 - me_c)

    barrier = pltpu.get_barrier_semaphore()

    def greet(device):
        pl.semaphore_signal(barrier, inc=1, device_id=device, device_id_type=pl.DeviceIdType.MESH)

    for chip in range(chips):
        for core in range(cores):
            to_chip, to_core = lax.rem(me_y + chip, chips), lax.rem(me_c + core, cores)
            device = (me_c, me_d, to_chip * cores + to_core)
            if chip or core:
                greet(device)
            else:
                pl.when(same == 0)(functools.partial(greet, device))
    pl.when(same == 0)(functools.partial(greet, core_dev))
    for step in range(1, depths):
        greet((me_f, lax.rem(me_d + step, depths), me_r))

    v_copy = pltpu.make_async_copy(v_hbm, raw, local_sem.at[0])
    v_copy.start()
    w_copy = pltpu.make_async_copy(w_hbm, wraw.at[me_c], local_sem.at[1])
    w_copy.start()
    region_copy = pltpu.make_async_copy(region_hbm, region, local_sem.at[2])
    region_copy.start()
    for part in range(2):
        slab[part, :depth_rows, :cols] = jnp.zeros((depth_rows, cols), jnp.bfloat16)
        slab[part, rows * depth_rows:, cols:] = jnp.zeros((depth_rows, cols), jnp.bfloat16)
    v_copy.wait()
    lanes_from_rows(raw, wide, pieces, vin)
    pl.semaphore_wait(barrier, frames * chips + depths - 1)

    def gather(part, index, device):
        return remote(vin.at[part], vol.at[part, me_r], g_send.at[part, index], g_recv.at[part, me_r], device)

    target = me_y * cores + me_f
    other_target = other_y * cores + me_f
    places = [(me_f, me_d, other_target), (other_f, me_d, other_target), (other_f, me_d, target)]
    volume_copies = [[gather(part, index, place) for index, place in enumerate(places)] for part in range(2)]
    core_copies = [gather(part, len(places), core_dev) for part in range(2)]

    def start_part(part):
        for copy in volume_copies[part]:
            copy.start()
        pl.when(same == 0)(core_copies[part].start)

    start_part(0)

    @pl.when(same == 1)
    def _():
        for part in range(2):
            vol[part, me_r] = vin[part]

    for frame in range(frames):
        for chip in range(chips):
            device = (lax.rem(me_f + frame, frames), me_d, lax.rem(me_y + chip, chips) * cores + me_f)
            if frame or chip:
                pl.semaphore_signal(ready, inc=1, device_id=device, device_id_type=pl.DeviceIdType.MESH)
            else:
                @pl.when(same == 0)
                def _():
                    pl.semaphore_signal(ready, inc=1, device_id=device, device_id_type=pl.DeviceIdType.MESH)
    w_copy.wait()
    w_send = remote(wraw.at[me_c], wraw.at[me_c], p_send, p_recv, core_dev)
    w_send.start()
    region_copy.wait()
    w_send.wait_recv()
    start_part(1)
    for tap_col in range(TAP_SIDE):
        bands = []
        for at in range(TAP_SIDE):
            tap = (TAP_SIDE - 1 - at) * TAP_SIDE + tap_col
            bands.append(jnp.concatenate([wraw[core, tap].astype(jnp.float32) for core in range(cores)], axis=0))
        wflat[tap_col * stack:(tap_col + 1) * stack, :] = jnp.concatenate(bands, axis=1).astype(jnp.bfloat16)

    lane = lax.broadcasted_iota(jnp.int32, (1, cols), 1)
    place = lax.rem(lane, side)
    row8 = lax.broadcasted_iota(jnp.int32, (8, cols), 0)
    lane_block = lax.broadcasted_iota(jnp.int32, (8, cols), 1) // col_share
    first_block = me_f * blocks_here

    def take(part):
        for source in range(row_shards):
            def arrive():
                remote(vin.at[0], vol.at[part, source], g_send.at[part, 0], g_recv.at[part, source], core_dev).wait_recv()
            pl.when((same == 0) | (source != me_r))(arrive)
        ids = region[...]
        crossed = pltpu.roll(ids, side, 1)
        ahead = pltpu.roll(crossed, rows - 1, 0)
        ahead = jnp.where(row8 < rows - 1, ahead, -1)
        low = lane < side
        owners = [jnp.where(low, ahead, ids) if part else jnp.where(low, ids, ahead)][0]
        before = jnp.where(low, crossed[:1], -1) if part else jnp.where(low, -1, crossed[:1])
        for at in range(-1, rows):
            slot = at // rows_here
            if at % rows_here == 0:
                data = vol[part, slot]
            else:
                prior, later = max(slot, 0), min(slot + 1, row_shards - 1)
                if part:
                    data = jnp.concatenate([vol[part, later][:, side:], vol[part, prior][:, :side]], axis=1)
                else:
                    data = jnp.concatenate([vol[part, prior][:, side:], vol[part, later][:, :side]], axis=1)
            owner = before if at < 0 else owners[at:at + 1]
            for block in range(blocks_here):
                keep = (owner == first_block + block).astype(jnp.float32).astype(jnp.bfloat16)
                kept = data * keep
                if at + reach <= rows:
                    top = (at + reach) * depth_rows + block * phases
                    slab[part, top:top + phases, :cols] = kept
                if at >= 0:
                    top = at * depth_rows + block * phases
                    slab[part, top:top + phases, cols:] = kept

    def multiply(part, group):
        top = group * rows // 2 * depth_rows
        cut = round_up(wflat.shape[0] // 2, 16)
        for low, high in ((0, cut), (cut, wflat.shape[0])):
            products[part, group, low:high, :] = jnp.dot(
                wflat[low:high, :], slab[part, top:top + TAP_SIDE * depth_rows, :], preferred_element_type=jnp.float32)

    def piece(part, pair, tap_col):
        left = pair % 2 * cols
        return products[part, pair // 2, tap_col * stack:(tap_col + 1) * stack, left:left + cols]

    def turn(value, shift):
        return pltpu.roll(value, shift % cols, 1)

    def emit(pair, total, shares):
        swapped = turn(total, side)
        upper, lower = (swapped, total) if shares[0] * col_share >= side else (total, swapped)
        peak = jnp.max(jnp.maximum(jnp.abs(upper), jnp.abs(lower)), axis=0, keepdims=True)
        code = jnp.ceil(8.0 * jnp.log2(jnp.maximum(peak, 1e-32)))
        inverse = LIMIT / jnp.exp2(code * 0.125)
        words = (jnp.round(upper * inverse).astype(jnp.int32) << 16) + jnp.round(lower * inverse).astype(jnp.int32)
        code = code.astype(jnp.int32)
        rest = words[depths * main:]
        for share in shares:
            start = share * col_share % side
            tile, extra = None, None
            for block in range(depths):
                shift = block * col_share - start
                moved = turn(words[block * main:(block + 1) * main], shift) if shift else words[block * main:(block + 1) * main]
                left = turn(rest, shift) if shift else rest
                tile = moved if tile is None else jnp.where(lane >= block * col_share, moved, tile)
                extra = left if extra is None else jnp.where(lane >= block * col_share, left, extra)
            extra = jnp.where(row8 // per == lane_block, extra, 0)
            step = 4
            while step >= per:
                extra = extra + pltpu.roll(extra, step, 0)
                step //= 2
            mark = jnp.where((lane >= start) & (lane < start + col_share), code, 0)
            mark = mark + turn(mark, cols // 2)
            mark = mark + turn(mark, cols // 4)
            outbox[pair, share, :main] = tile
            outbox[pair, share, main:main + per] = extra[:per]
            outbox[pair, share, main + per:] = mark

    def pack_first(pair):
        total = None
        for tap_col in range(TAP_SIDE):
            shift = tap_col - reach
            term = piece(0, pair, tap_col)
            if shift > 0:
                term = turn(jnp.where(place < side - shift, term, 0.0), shift)
            if shift < 0:
                term = turn(jnp.where(place >= -shift, term, 0.0), shift)
            total = term if total is None else total + term
        sums[pair] = total
        emit(pair, total, (0,))

    def pack_second(pair):
        near, far = sums[pair], None
        for tap_col in range(TAP_SIDE):
            shift = tap_col - reach
            term = piece(1, pair, tap_col)
            if shift > 0:
                term = turn(jnp.where(place < side - shift, term, piece(0, pair, tap_col)), shift)
            if shift < 0:
                near = near + turn(jnp.where(place < -shift, term, 0.0), shift)
                term = turn(jnp.where(place < -shift, 0.0, term), shift)
            far = term if far is None else far + term
        emit(pair, near, (1,))
        emit(pair, far, (2, 3))

    def message(index, share, pair, device_d):
        return remote(outbox.at[index, share], inbox.at[me_y, me_f, me_d], m_send.at[index, share],
                      m_recv.at[me_y, me_f, me_d], (me_c, device_d, pair))

    def each_message(pairs, shares, act, stay=None):
        for share in shares:
            for pair in pairs:
                copy = message(pair, share, pair, share)
                own = same * (me_r == pair).astype(jnp.int32) * (me_d == share).astype(jnp.int32)
                pl.when(own == 0)(functools.partial(act, copy))
                if stay is not None:
                    pl.when(own == 1)(functools.partial(stay, pair, share))

    def keep_own(pair, share):
        inbox[me_y, me_f, me_d] = outbox[pair, share]

    def send(pairs, shares):
        each_message(pairs, shares, lambda copy: copy.start(), keep_own)

    take(0)
    multiply(0, 0)
    multiply(0, 1)
    pack_first(0)
    pack_first(1)
    pl.semaphore_wait(ready, row_shards - same)
    send((0, 1), (0,))
    pack_first(2)
    pack_first(3)
    send((2, 3), (0,))
    take(1)
    multiply(1, 0)
    multiply(1, 1)
    pack_second(0)
    pack_second(1)
    send((0, 1), range(1, depths))
    pack_second(2)
    pack_second(3)
    send((2, 3), range(1, depths))
    received = [[None] * rows_here for _ in range(chips)]
    for frame_step in range(frames):
        frame = lax.rem(me_f + frame_step, frames)
        for step in range(depths):
            for chip in range(chips):
                depth = lax.rem(me_d + step, depths)

                def arrive():
                    remote(outbox.at[0, 0], inbox.at[chip, frame, depth], m_send.at[0, 0],
                           m_recv.at[chip, frame, depth], core_dev).wait_recv()
                if frame_step or step:
                    arrive()
                else:
                    pl.when((same == 0) | (chip != me_y))(arrive)
                block = inbox[chip, frame, depth]
                scale = jnp.exp2(block[main + per:].astype(jnp.float32) * 0.125) * (1.0 / LIMIT)
                lower = (block << 16) >> 16
                upper = (block - lower).astype(jnp.float32) * (scale * (1.0 / 65536.0))
                lower = lower.astype(jnp.float32) * scale
                received[chip] = [
                    term if held is None else held + term for held, term in zip(received[chip], (upper, lower))]
    halves = []
    for total in received:
        extra_rows = []
        for block in range(depths):
            moved = []
            for row in range(rows_here):
                shift = (row - block) * col_share % cols
                moved.append(pltpu.roll(total[row], shift, 1) if shift else total[row])
            merged = jnp.where(lane < col_share, moved[0], moved[1])
            halves.append(merged[:main])
            extra_rows.append(merged[main:main + per])
        halves.append(jnp.concatenate(extra_rows, axis=0))
    lanes_here = rows_here * col_share
    turned = jnp.concatenate(halves, axis=0).T[:lanes_here]
    group = math.lcm(phases, 128) // phases
    span = group * phases
    per_row = col_share // group
    members = []
    for half in range(pieces.shape[0]):
        count = min(128, phases - half * 128)
        pieces[half, :lanes_here, :count] = turned[:, half * 128:half * 128 + count]
    for member in range(group):
        for half in range(pieces.shape[0]):
            count = min(128, phases - half * 128)
            members.append(pieces[half, pl.ds(member, rows_here * per_row, stride=group), :][:, :count])
    strips = jnp.concatenate(members, axis=1)
    for row in range(rows_here):
        for at in range(per_row):
            line = row * per_row + at
            cam[row:row + 1, at * span:(at + 1) * span] = strips[line:line + 1]
    for part in range(2):
        for copy in volume_copies[part]:
            copy.wait_send()
        pl.when(same == 0)(core_copies[part].wait_send)
    w_send.wait_send()
    each_message(range(row_shards), range(depths), lambda copy: copy.wait_send())


def hand_over(camera_in, recorded, weight, camera_out, residual_out):
    camera_out[...] = camera_in[...]
    residual_out[...] = weight[...].astype(jnp.float32) * (camera_in[...] - recorded[...].astype(jnp.float32))


def fused_body(sizes, volume, point_spread, region_map, measured, pixel_weight):
    frames, depths, row_shards = sizes
    _, _, rows_here, merged = volume.shape
    cols = merged // PHASES
    _, depth_rows, taps, width = point_spread.shape
    rows = rows_here * row_shards
    stack = CORES * width
    lines = stack // depths + 1
    group = math.lcm(PHASES, 128) // PHASES
    span = group * PHASES
    image = (rows_here, cols // depths * PHASES)
    spread = point_spread.reshape(depth_rows, taps, width).transpose(1, 2, 0)
    vmem = pl.BlockSpec(memory_space=pltpu.VMEM)
    hbm = pl.BlockSpec(memory_space=pltpu.HBM)
    dma = pltpu.SemaphoreType.DMA
    camera = pl.pallas_call(
        functools.partial(kernel, frames, depths, row_shards),
        out_shape=jax.ShapeDtypeStruct(image, jnp.float32),
        in_specs=[hbm, hbm, hbm],
        out_specs=vmem,
        scratch_shapes=[
            pltpu.VMEM((rows_here, merged), jnp.bfloat16),
            pltpu.VMEM((rows_here * cols // group, span + 128), jnp.float32),
            pltpu.VMEM((round_up(PHASES, 128) // 128, rows_here * cols, 128), jnp.float32),
            pltpu.VMEM((2, PHASES, cols), jnp.bfloat16),
            pltpu.VMEM(region_map.shape, jnp.int32),
            pltpu.VMEM((2, row_shards, PHASES, cols), jnp.bfloat16),
            pltpu.VMEM((CORES, taps, width, depth_rows), jnp.bfloat16),
            pltpu.VMEM((TAP_SIDE * stack, TAP_SIDE * depth_rows), jnp.bfloat16),
            pltpu.VMEM((2, (rows + 1) * depth_rows, rows_here * cols), jnp.bfloat16),
            pltpu.VMEM((2, 2, TAP_SIDE * stack, rows_here * cols), jnp.float32),
            pltpu.VMEM((row_shards, stack, cols), jnp.float32),
            pltpu.VMEM((row_shards, depths, lines, cols), jnp.int32),
            pltpu.VMEM((row_shards // CORES, frames, depths, lines, cols), jnp.int32),
            pltpu.SemaphoreType.REGULAR, dma((3,)), dma((2, 4)), dma((2, row_shards)), dma, dma, dma((row_shards, depths)),
            dma((row_shards // CORES, frames, depths)),
        ],
        compiler_params=pltpu.CompilerParams(collective_id=0, has_side_effects=True, vmem_limit_bytes=24 << 20),
    )(*[pltpu.with_memory_space_constraint(each, pltpu.HBM) for each in (volume.reshape(rows_here, merged), spread, region_map)])
    camera, residual = pl.pallas_call(
        hand_over,
        out_shape=[jax.ShapeDtypeStruct(image, jnp.float32)] * 2,
        in_specs=[vmem] * 3,
        out_specs=[vmem, vmem],
        compiler_params=pltpu.CompilerParams(vmem_limit_bytes=4 << 20),
    )(camera, measured.reshape(image), pixel_weight.reshape(image))
    return (camera.reshape(measured.shape), residual.reshape(measured.shape))


def solution(mesh):
    in_specs = (
        P("depth", "frame", "row", None),
        P("depth", "frame", None, "row"),
        P(),
        P("frame", "row", "depth"),
        P("frame", "row", "depth"),
    )
    out_specs = (P("frame", "row", "depth"), P("frame", "row", "depth"))
    sizes = (mesh.shape["frame"], mesh.shape["depth"], mesh.shape["row"])

    def body(volume, *rest):
        blocks_fit = rest[0].shape[1] % PHASES == 0
        stack = CORES * rest[0].shape[3]
        packs = sizes[1] == 4 and stack % 8 == 0 and stack // 8 % sizes[1] == 1
        pairs = volume.shape[2] == 2 and (volume.shape[3] // PHASES) == 128
        if sizes[0] == 2 and sizes[2] == 2 * CORES and volume.shape[1] == 1 and blocks_fit and packs and pairs:
            return fused_body(sizes, volume, *rest)
        return plain_body(volume, *rest)

    return jax.shard_map(body, mesh=mesh, in_specs=in_specs, out_specs=out_specs, check_vma=False)
```

```python
import functools
import math

import jax
import jax.numpy as jnp
from jax import lax
from jax.experimental import pallas as pl
from jax.experimental.pallas import tpu as pltpu
from jax.sharding import PartitionSpec as P

PHASES = 144
BLOCKS = 4
TAP_SIDE = 5
CORES = 2
LIMIT = 32000.0


def build_taps(planes, region_rows):
    tap_reach = TAP_SIDE // 2
    frames, row_count, merged = planes.shape
    col_count = merged // PHASES
    split_planes = planes.reshape(frames, row_count, col_count, PHASES)
    block_ids = jnp.arange(BLOCKS, dtype=jnp.int32)
    onehot = (region_rows[:, :, None] == block_ids[None, None, :]).astype(jnp.bfloat16)
    expanded = (split_planes[:, :, :, None, :] * onehot[None, :, :, :, None]).reshape(
        frames, row_count, col_count, BLOCKS * PHASES
    )
    return jnp.pad(expanded, ((0, 0), (0, 0), (tap_reach, tap_reach), (0, 0)))


def project(padded, spread_local, out_rows):
    tap_reach = TAP_SIDE // 2
    frames, ext_rows, ext_cols, _ = padded.shape
    col_count = ext_cols - 2 * tap_reach
    out_width = spread_local.shape[2]
    zero_start = jnp.zeros((frames * out_rows * col_count, out_width), jnp.float32)
    running = zero_start
    spread_slab = lax.all_gather(spread_local, "frame", axis=0, tiled=True)
    piece_rows = spread_slab.shape[0]
    flat_cols = padded.reshape(frames * ext_rows * ext_cols, piece_rows)
    for tap_row in range(TAP_SIDE):
        row_taps = spread_slab[:, tap_row * TAP_SIDE : (tap_row + 1) * TAP_SIDE, :].reshape(
            piece_rows, TAP_SIDE * out_width
        )
        product = jnp.dot(flat_cols, row_taps, preferred_element_type=jnp.float32)
        product = product.reshape(frames, ext_rows, ext_cols, TAP_SIDE, out_width)
        first_row = 2 * tap_reach - tap_row
        for tap_col in range(TAP_SIDE):
            first_col = 2 * tap_reach - tap_col
            shifted = product[
                :, first_row : first_row + out_rows, first_col : first_col + col_count, tap_col, :
            ]
            running = running + shifted.reshape(frames * out_rows * col_count, out_width)
    partial_value = running.reshape(frames, out_rows, col_count * out_width)
    return lax.psum_scatter(partial_value, "depth", scatter_dimension=2, tiled=True)


def plain_body(volume, point_spread, region_map, measured, pixel_weight):
    tap_reach = TAP_SIDE // 2
    planes = volume[0]
    row_count = planes.shape[1]
    region_padded = jnp.pad(region_map, ((tap_reach, tap_reach), (0, 0)), constant_values=-1)
    all_rows = lax.all_gather(planes, "row", axis=1, tiled=True)
    extended = jnp.pad(all_rows, ((0, 0), (tap_reach, tap_reach), (0, 0)))
    padded = build_taps(extended, region_padded)
    piece_width = point_spread.shape[3]
    partial_value = project(padded, point_spread[0], all_rows.shape[1])
    frames, total_rows, merged = partial_value.shape
    split_partial = partial_value.reshape(frames, total_rows, merged // piece_width, piece_width)
    returned = lax.all_to_all(split_partial, "row", split_axis=1, concat_axis=3, tiled=True)
    camera = returned.reshape(frames, row_count, returned.shape[2] * returned.shape[3])
    residual = pixel_weight.astype(jnp.float32) * (camera - measured.astype(jnp.float32))
    return (camera, residual)


def round_up(value, step):
    return (value + step - 1) // step * step


def remote(src, dst, send_sem, recv_sem, device):
    return pltpu.make_async_remote_copy(
        src_ref=src, dst_ref=dst, send_sem=send_sem, recv_sem=recv_sem,
        device_id=device, device_id_type=pl.DeviceIdType.MESH,
    )


def lanes_from_rows(raw, wide, pieces, vin):
    _, phases, cols = vin.shape
    rows_here = raw.shape[0]
    group = math.lcm(phases, 128) // phases
    span = group * phases
    groups = cols // group
    wide[:, span:] = jnp.zeros((wide.shape[0], wide.shape[1] - span), jnp.float32)
    for at in range(groups):
        strip = raw[:, at * span:(at + 1) * span].astype(jnp.float32)
        for row in range(rows_here):
            wide[row * groups + at:row * groups + at + 1, :span] = strip[row:row + 1]
    for member in range(group):
        for half in range(pieces.shape[0]):
            first = member * phases + half * 128
            pieces[half, pl.ds(member, rows_here * groups, stride=group), :] = wide[:, first:first + 128]
    side = cols // 2
    for part in range(2):
        for half in range(pieces.shape[0]):
            count = min(128, phases - half * 128)
            rows = [pieces[half, row * cols + part * side:row * cols + (part + 1) * side, :] for row in range(rows_here)]
            turned = jnp.concatenate(rows[::-1] if part else rows, axis=0).T
            vin[part, half * 128:half * 128 + count, :] = turned[:count].astype(jnp.bfloat16)


def kernel(frames, depths, row_shards, v_hbm, w_hbm, region_hbm, cam, raw, wide, pieces, vin, region, vol, wraw,
           wflat, slab, products, sums, outbox, inbox, ready, local_sem, g_send, g_recv, p_send, p_recv, m_send, m_recv):
    reach = TAP_SIDE // 2
    _, phases, cols = vin.shape
    rows_here = raw.shape[0]
    side = cols // 2
    rows = rows_here * row_shards
    cores, taps, width, depth_rows = wraw.shape
    chips = row_shards // cores
    blocks_here = depth_rows // phases
    stack = cores * width
    col_share = cols // depths
    main = stack // (8 * depths) * 8
    per = 8 // depths
    me_f, me_d, me_r = lax.axis_index("frame"), lax.axis_index("depth"), lax.axis_index("row")
    me_y, me_c = me_r // cores, lax.rem(me_r, cores)
    other_f, other_y = 1 - me_f, 1 - me_y
    same = 1 - lax.rem(me_f + me_c, 2)
    core_dev = (me_f, me_d, me_y * cores + 1 - me_c)

    barrier = pltpu.get_barrier_semaphore()

    def greet(device):
        pl.semaphore_signal(barrier, inc=1, device_id=device, device_id_type=pl.DeviceIdType.MESH)

    for chip in range(chips):
        for core in range(cores):
            to_chip, to_core = lax.rem(me_y + chip, chips), lax.rem(me_c + core, cores)
            device = (me_c, me_d, to_chip * cores + to_core)
            if chip or core:
                greet(device)
            else:
                pl.when(same == 0)(functools.partial(greet, device))
    pl.when(same == 0)(functools.partial(greet, core_dev))
    for step in range(1, depths):
        greet((me_f, lax.rem(me_d + step, depths), me_r))

    v_copy = pltpu.make_async_copy(v_hbm, raw, local_sem.at[0])
    v_copy.start()
    w_copy = pltpu.make_async_copy(w_hbm, wraw.at[me_c], local_sem.at[1])
    w_copy.start()
    region_copy = pltpu.make_async_copy(region_hbm, region, local_sem.at[2])
    region_copy.start()
    for part in range(2):
        slab[part, :depth_rows, :cols] = jnp.zeros((depth_rows, cols), jnp.bfloat16)
        slab[part, rows * depth_rows:, cols:] = jnp.zeros((depth_rows, cols), jnp.bfloat16)
    v_copy.wait()
    lanes_from_rows(raw, wide, pieces, vin)
    pl.semaphore_wait(barrier, frames * chips + depths - 1)

    def gather(part, index, device):
        return remote(vin.at[part], vol.at[part, me_r], g_send.at[part, index], g_recv.at[part, me_r], device)

    target = me_y * cores + me_f
    other_target = other_y * cores + me_f
    places = [(other_f, me_d, (chips - 1) * cores + me_f), (other_f, me_d, me_f), (me_f, me_d, other_target)]
    volume_copies = [[gather(part, index, place) for index, place in enumerate(places)] for part in range(2)]
    core_copies = [gather(part, len(places), core_dev) for part in range(2)]

    def start_part(part):
        for copy in volume_copies[part]:
            copy.start()
        pl.when(same == 0)(core_copies[part].start)

    start_part(0)

    @pl.when(same == 1)
    def _():
        for part in range(2):
            vol[part, me_r] = vin[part]

    for frame in range(frames):
        for chip in range(chips):
            device = (lax.rem(me_f + frame, frames), me_d, lax.rem(me_y + chip, chips) * cores + me_f)
            if frame or chip:
                pl.semaphore_signal(ready, inc=1, device_id=device, device_id_type=pl.DeviceIdType.MESH)
            else:
                @pl.when(same == 0)
                def _():
                    pl.semaphore_signal(ready, inc=1, device_id=device, device_id_type=pl.DeviceIdType.MESH)
    w_copy.wait()
    w_send = remote(wraw.at[me_c], wraw.at[me_c], p_send, p_recv, core_dev)
    w_send.start()
    region_copy.wait()
    w_send.wait_recv()
    start_part(1)
    for tap_col in range(TAP_SIDE):
        bands = []
        for at in range(TAP_SIDE):
            tap = (TAP_SIDE - 1 - at) * TAP_SIDE + tap_col
            bands.append(jnp.concatenate([wraw[core, tap].astype(jnp.float32) for core in range(cores)], axis=0))
        wflat[tap_col * stack:(tap_col + 1) * stack, :] = jnp.concatenate(bands, axis=1).astype(jnp.bfloat16)

    lane = lax.broadcasted_iota(jnp.int32, (1, cols), 1)
    place = lax.rem(lane, side)
    row8 = lax.broadcasted_iota(jnp.int32, (8, cols), 0)
    lane_block = lax.broadcasted_iota(jnp.int32, (8, cols), 1) // col_share
    first_block = me_f * blocks_here

    def take(part):
        for source in range(row_shards):
            def arrive():
                remote(vin.at[0], vol.at[part, source], g_send.at[part, 0], g_recv.at[part, source], core_dev).wait_recv()
            pl.when((same == 0) | (source != me_r))(arrive)
        ids = region[...]
        crossed = pltpu.roll(ids, side, 1)
        ahead = pltpu.roll(crossed, rows - 1, 0)
        ahead = jnp.where(row8 < rows - 1, ahead, -1)
        low = lane < side
        owners = [jnp.where(low, ahead, ids) if part else jnp.where(low, ids, ahead)][0]
        before = jnp.where(low, crossed[:1], -1) if part else jnp.where(low, -1, crossed[:1])
        for at in range(-1, rows):
            slot = at // rows_here
            if at % rows_here == 0:
                data = vol[part, slot]
            else:
                prior, later = max(slot, 0), min(slot + 1, row_shards - 1)
                if part:
                    data = jnp.concatenate([vol[part, later][:, side:], vol[part, prior][:, :side]], axis=1)
                else:
                    data = jnp.concatenate([vol[part, prior][:, side:], vol[part, later][:, :side]], axis=1)
            owner = before if at < 0 else owners[at:at + 1]
            for block in range(blocks_here):
                keep = (owner == first_block + block).astype(jnp.float32).astype(jnp.bfloat16)
                kept = data * keep
                if at + reach <= rows:
                    top = (at + reach) * depth_rows + block * phases
                    slab[part, top:top + phases, :cols] = kept
                if at >= 0:
                    top = at * depth_rows + block * phases
                    slab[part, top:top + phases, cols:] = kept

    def multiply(part, group):
        top = group * rows // 2 * depth_rows
        cut = round_up(wflat.shape[0] // 2, 16)
        for low, high in ((0, cut), (cut, wflat.shape[0])):
            products[part, group, low:high, :] = jnp.dot(
                wflat[low:high, :], slab[part, top:top + TAP_SIDE * depth_rows, :], preferred_element_type=jnp.float32)

    def piece(part, pair, tap_col):
        left = pair % 2 * cols
        return products[part, pair // 2, tap_col * stack:(tap_col + 1) * stack, left:left + cols]

    def turn(value, shift):
        return pltpu.roll(value, shift % cols, 1)

    def emit(pair, total, shares):
        swapped = turn(total, side)
        upper, lower = (swapped, total) if shares[0] * col_share >= side else (total, swapped)
        peak = jnp.max(jnp.maximum(jnp.abs(upper), jnp.abs(lower)), axis=0, keepdims=True)
        code = jnp.ceil(8.0 * jnp.log2(jnp.maximum(peak, 1e-32)))
        inverse = LIMIT / jnp.exp2(code * 0.125)
        words = (jnp.round(upper * inverse).astype(jnp.int32) << 16) + jnp.round(lower * inverse).astype(jnp.int32)
        code = code.astype(jnp.int32)
        rest = words[depths * main:]
        for share in shares:
            start = share * col_share % side
            tile, extra = None, None
            for block in range(depths):
                shift = block * col_share - start
                moved = turn(words[block * main:(block + 1) * main], shift) if shift else words[block * main:(block + 1) * main]
                left = turn(rest, shift) if shift else rest
                tile = moved if tile is None else jnp.where(lane >= block * col_share, moved, tile)
                extra = left if extra is None else jnp.where(lane >= block * col_share, left, extra)
            extra = jnp.where(row8 // per == lane_block, extra, 0)
            step = 4
            while step >= per:
                extra = extra + pltpu.roll(extra, step, 0)
                step //= 2
            mark = jnp.where((lane >= start) & (lane < start + col_share), code, 0)
            mark = mark + turn(mark, cols // 2)
            mark = mark + turn(mark, cols // 4)
            outbox[pair, share, :main] = tile
            outbox[pair, share, main:main + per] = extra[:per]
            outbox[pair, share, main + per:] = mark

    def pack_first(pair):
        total = None
        for tap_col in range(TAP_SIDE):
            shift = tap_col - reach
            term = piece(0, pair, tap_col)
            if shift > 0:
                term = turn(jnp.where(place < side - shift, term, 0.0), shift)
            if shift < 0:
                term = turn(jnp.where(place >= -shift, term, 0.0), shift)
            total = term if total is None else total + term
        sums[pair] = total
        emit(pair, total, (0,))

    def pack_second(pair):
        near, far = sums[pair], None
        for tap_col in range(TAP_SIDE):
            shift = tap_col - reach
            term = piece(1, pair, tap_col)
            if shift > 0:
                term = turn(jnp.where(place < side - shift, term, piece(0, pair, tap_col)), shift)
            if shift < 0:
                near = near + turn(jnp.where(place < -shift, term, 0.0), shift)
                term = turn(jnp.where(place < -shift, 0.0, term), shift)
            far = term if far is None else far + term
        emit(pair, near, (1,))
        emit(pair, far, (2, 3))

    def message(index, share, pair, device_d):
        return remote(outbox.at[index, share], inbox.at[me_y, me_f, me_d], m_send.at[index, share],
                      m_recv.at[me_y, me_f, me_d], (me_c, device_d, pair))

    def each_message(pairs, shares, act, stay=None):
        for share in shares:
            for pair in pairs:
                copy = message(pair, share, pair, share)
                own = same * (me_r == pair).astype(jnp.int32) * (me_d == share).astype(jnp.int32)
                pl.when(own == 0)(functools.partial(act, copy))
                if stay is not None:
                    pl.when(own == 1)(functools.partial(stay, pair, share))

    def keep_own(pair, share):
        inbox[me_y, me_f, me_d] = outbox[pair, share]

    def send(pairs, shares):
        each_message(pairs, shares, lambda copy: copy.start(), keep_own)

    pl.semaphore_wait(ready, row_shards - same)
    take(0)
    multiply(0, 0)
    pack_first(0)
    pack_first(1)
    send((0, 1), (0,))
    multiply(0, 1)
    pack_first(2)
    pack_first(3)
    send((2, 3), (0,))
    take(1)
    multiply(1, 0)
    multiply(1, 1)
    pack_second(0)
    pack_second(1)
    send((0, 1), range(1, depths))
    pack_second(2)
    pack_second(3)
    send((2, 3), range(1, depths))
    received = [[None] * rows_here for _ in range(chips)]
    for frame_step in range(frames):
        frame = lax.rem(me_f + frame_step, frames)
        for step in range(depths):
            for chip in range(chips):
                depth = lax.rem(me_d + step, depths)

                def arrive():
                    remote(outbox.at[0, 0], inbox.at[chip, frame, depth], m_send.at[0, 0],
                           m_recv.at[chip, frame, depth], core_dev).wait_recv()
                if frame_step or step:
                    arrive()
                else:
                    pl.when((same == 0) | (chip != me_y))(arrive)
                block = inbox[chip, frame, depth]
                scale = jnp.exp2(block[main + per:].astype(jnp.float32) * 0.125) * (1.0 / LIMIT)
                lower = (block << 16) >> 16
                upper = (block - lower).astype(jnp.float32) * (scale * (1.0 / 65536.0))
                lower = lower.astype(jnp.float32) * scale
                received[chip] = [
                    term if held is None else held + term for held, term in zip(received[chip], (upper, lower))]
    halves = []
    for total in received:
        extra_rows = []
        for block in range(depths):
            moved = []
            for row in range(rows_here):
                shift = (row - block) * col_share % cols
                moved.append(pltpu.roll(total[row], shift, 1) if shift else total[row])
            merged = jnp.where(lane < col_share, moved[0], moved[1])
            halves.append(merged[:main])
            extra_rows.append(merged[main:main + per])
        halves.append(jnp.concatenate(extra_rows, axis=0))
    lanes_here = rows_here * col_share
    turned = jnp.concatenate(halves, axis=0).T[:lanes_here]
    group = math.lcm(phases, 128) // phases
    span = group * phases
    per_row = col_share // group
    members = []
    for half in range(pieces.shape[0]):
        count = min(128, phases - half * 128)
        pieces[half, :lanes_here, :count] = turned[:, half * 128:half * 128 + count]
    for member in range(group):
        for half in range(pieces.shape[0]):
            count = min(128, phases - half * 128)
            members.append(pieces[half, pl.ds(member, rows_here * per_row, stride=group), :][:, :count])
    strips = jnp.concatenate(members, axis=1)
    for row in range(rows_here):
        for at in range(per_row):
            line = row * per_row + at
            cam[row:row + 1, at * span:(at + 1) * span] = strips[line:line + 1]
    for part in range(2):
        for copy in volume_copies[part]:
            copy.wait_send()
        pl.when(same == 0)(core_copies[part].wait_send)
    w_send.wait_send()
    each_message(range(row_shards), range(depths), lambda copy: copy.wait_send())


def hand_over(camera_in, recorded, weight, camera_out, residual_out):
    camera_out[...] = camera_in[...]
    residual_out[...] = weight[...].astype(jnp.float32) * (camera_in[...] - recorded[...].astype(jnp.float32))


def fused_body(sizes, volume, point_spread, region_map, measured, pixel_weight):
    frames, depths, row_shards = sizes
    _, _, rows_here, merged = volume.shape
    cols = merged // PHASES
    _, depth_rows, taps, width = point_spread.shape
    rows = rows_here * row_shards
    stack = CORES * width
    lines = stack // depths + 1
    group = math.lcm(PHASES, 128) // PHASES
    span = group * PHASES
    image = (rows_here, cols // depths * PHASES)
    spread = point_spread.reshape(depth_rows, taps, width).transpose(1, 2, 0)
    vmem = pl.BlockSpec(memory_space=pltpu.VMEM)
    hbm = pl.BlockSpec(memory_space=pltpu.HBM)
    dma = pltpu.SemaphoreType.DMA
    camera = pl.pallas_call(
        functools.partial(kernel, frames, depths, row_shards),
        out_shape=jax.ShapeDtypeStruct(image, jnp.float32),
        in_specs=[hbm, hbm, hbm],
        out_specs=vmem,
        scratch_shapes=[
            pltpu.VMEM((rows_here, merged), jnp.bfloat16),
            pltpu.VMEM((rows_here * cols // group, span + 128), jnp.float32),
            pltpu.VMEM((round_up(PHASES, 128) // 128, rows_here * cols, 128), jnp.float32),
            pltpu.VMEM((2, PHASES, cols), jnp.bfloat16),
            pltpu.VMEM(region_map.shape, jnp.int32),
            pltpu.VMEM((2, row_shards, PHASES, cols), jnp.bfloat16),
            pltpu.VMEM((CORES, taps, width, depth_rows), jnp.bfloat16),
            pltpu.VMEM((TAP_SIDE * stack, TAP_SIDE * depth_rows), jnp.bfloat16),
            pltpu.VMEM((2, (rows + 1) * depth_rows, rows_here * cols), jnp.bfloat16),
            pltpu.VMEM((2, 2, TAP_SIDE * stack, rows_here * cols), jnp.float32),
            pltpu.VMEM((row_shards, stack, cols), jnp.float32),
            pltpu.VMEM((row_shards, depths, lines, cols), jnp.int32),
            pltpu.VMEM((row_shards // CORES, frames, depths, lines, cols), jnp.int32),
            pltpu.SemaphoreType.REGULAR, dma((3,)), dma((2, 4)), dma((2, row_shards)), dma, dma, dma((row_shards, depths)),
            dma((row_shards // CORES, frames, depths)),
        ],
        compiler_params=pltpu.CompilerParams(collective_id=0, has_side_effects=True, vmem_limit_bytes=24 << 20),
    )(*[pltpu.with_memory_space_constraint(each, pltpu.HBM) for each in (volume.reshape(rows_here, merged), spread, region_map)])
    camera, residual = pl.pallas_call(
        hand_over,
        out_shape=[jax.ShapeDtypeStruct(image, jnp.float32)] * 2,
        in_specs=[vmem] * 3,
        out_specs=[vmem, vmem],
        compiler_params=pltpu.CompilerParams(vmem_limit_bytes=4 << 20),
    )(camera, measured.reshape(image), pixel_weight.reshape(image))
    return (camera.reshape(measured.shape), residual.reshape(measured.shape))


def solution(mesh):
    in_specs = (
        P("depth", "frame", "row", None),
        P("depth", "frame", None, "row"),
        P(),
        P("frame", "row", "depth"),
        P("frame", "row", "depth"),
    )
    out_specs = (P("frame", "row", "depth"), P("frame", "row", "depth"))
    sizes = (mesh.shape["frame"], mesh.shape["depth"], mesh.shape["row"])

    def body(volume, *rest):
        blocks_fit = rest[0].shape[1] % PHASES == 0
        stack = CORES * rest[0].shape[3]
        packs = sizes[1] == 4 and stack % 8 == 0 and stack // 8 % sizes[1] == 1
        pairs = volume.shape[2] == 2 and (volume.shape[3] // PHASES) == 128
        if sizes[0] == 2 and sizes[2] == 2 * CORES and volume.shape[1] == 1 and blocks_fit and packs and pairs:
            return fused_body(sizes, volume, *rest)
        return plain_body(volume, *rest)

    return jax.shard_map(body, mesh=mesh, in_specs=in_specs, out_specs=out_specs, check_vma=False)
```

```python
import functools
import math

import jax
import jax.numpy as jnp
from jax import lax
from jax.experimental import pallas as pl
from jax.experimental.pallas import tpu as pltpu
from jax.sharding import PartitionSpec as P

PHASES = 144
BLOCKS = 4
TAP_SIDE = 5
CORES = 2
LIMIT = 32000.0


def build_taps(planes, region_rows):
    tap_reach = TAP_SIDE // 2
    frames, row_count, merged = planes.shape
    col_count = merged // PHASES
    split_planes = planes.reshape(frames, row_count, col_count, PHASES)
    block_ids = jnp.arange(BLOCKS, dtype=jnp.int32)
    onehot = (region_rows[:, :, None] == block_ids[None, None, :]).astype(jnp.bfloat16)
    expanded = (split_planes[:, :, :, None, :] * onehot[None, :, :, :, None]).reshape(
        frames, row_count, col_count, BLOCKS * PHASES
    )
    return jnp.pad(expanded, ((0, 0), (0, 0), (tap_reach, tap_reach), (0, 0)))


def project(padded, spread_local, out_rows):
    tap_reach = TAP_SIDE // 2
    frames, ext_rows, ext_cols, _ = padded.shape
    col_count = ext_cols - 2 * tap_reach
    out_width = spread_local.shape[2]
    zero_start = jnp.zeros((frames * out_rows * col_count, out_width), jnp.float32)
    running = zero_start
    spread_slab = lax.all_gather(spread_local, "frame", axis=0, tiled=True)
    piece_rows = spread_slab.shape[0]
    flat_cols = padded.reshape(frames * ext_rows * ext_cols, piece_rows)
    for tap_row in range(TAP_SIDE):
        row_taps = spread_slab[:, tap_row * TAP_SIDE : (tap_row + 1) * TAP_SIDE, :].reshape(
            piece_rows, TAP_SIDE * out_width
        )
        product = jnp.dot(flat_cols, row_taps, preferred_element_type=jnp.float32)
        product = product.reshape(frames, ext_rows, ext_cols, TAP_SIDE, out_width)
        first_row = 2 * tap_reach - tap_row
        for tap_col in range(TAP_SIDE):
            first_col = 2 * tap_reach - tap_col
            shifted = product[
                :, first_row : first_row + out_rows, first_col : first_col + col_count, tap_col, :
            ]
            running = running + shifted.reshape(frames * out_rows * col_count, out_width)
    partial_value = running.reshape(frames, out_rows, col_count * out_width)
    return lax.psum_scatter(partial_value, "depth", scatter_dimension=2, tiled=True)


def plain_body(volume, point_spread, region_map, measured, pixel_weight):
    tap_reach = TAP_SIDE // 2
    planes = volume[0]
    row_count = planes.shape[1]
    region_padded = jnp.pad(region_map, ((tap_reach, tap_reach), (0, 0)), constant_values=-1)
    all_rows = lax.all_gather(planes, "row", axis=1, tiled=True)
    extended = jnp.pad(all_rows, ((0, 0), (tap_reach, tap_reach), (0, 0)))
    padded = build_taps(extended, region_padded)
    piece_width = point_spread.shape[3]
    partial_value = project(padded, point_spread[0], all_rows.shape[1])
    frames, total_rows, merged = partial_value.shape
    split_partial = partial_value.reshape(frames, total_rows, merged // piece_width, piece_width)
    returned = lax.all_to_all(split_partial, "row", split_axis=1, concat_axis=3, tiled=True)
    camera = returned.reshape(frames, row_count, returned.shape[2] * returned.shape[3])
    residual = pixel_weight.astype(jnp.float32) * (camera - measured.astype(jnp.float32))
    return (camera, residual)


def round_up(value, step):
    return (value + step - 1) // step * step


def remote(src, dst, send_sem, recv_sem, device):
    return pltpu.make_async_remote_copy(
        src_ref=src, dst_ref=dst, send_sem=send_sem, recv_sem=recv_sem,
        device_id=device, device_id_type=pl.DeviceIdType.MESH,
    )


def lanes_from_rows(raw, wide, pieces, vin):
    _, phases, cols = vin.shape
    rows_here = raw.shape[0]
    group = math.lcm(phases, 128) // phases
    span = group * phases
    groups = cols // group
    wide[:, span:] = jnp.zeros((wide.shape[0], wide.shape[1] - span), jnp.float32)
    for at in range(groups):
        strip = raw[:, at * span:(at + 1) * span].astype(jnp.float32)
        for row in range(rows_here):
            wide[row * groups + at:row * groups + at + 1, :span] = strip[row:row + 1]
    for member in range(group):
        for half in range(pieces.shape[0]):
            first = member * phases + half * 128
            pieces[half, pl.ds(member, rows_here * groups, stride=group), :] = wide[:, first:first + 128]
    side = cols // 2
    for part in range(2):
        for half in range(pieces.shape[0]):
            count = min(128, phases - half * 128)
            rows = [pieces[half, row * cols + part * side:row * cols + (part + 1) * side, :] for row in range(rows_here)]
            turned = jnp.concatenate(rows[::-1] if part else rows, axis=0).T
            vin[part, half * 128:half * 128 + count, :] = turned[:count].astype(jnp.bfloat16)


def kernel(frames, depths, row_shards, v_hbm, w_hbm, region_hbm, cam, raw, wide, pieces, vin, region, vol, wraw,
           wflat, slab, products, sums, outbox, inbox, ready, local_sem, g_send, g_recv, p_send, p_recv, m_send, m_recv):
    reach = TAP_SIDE // 2
    _, phases, cols = vin.shape
    rows_here = raw.shape[0]
    side = cols // 2
    rows = rows_here * row_shards
    cores, taps, width, depth_rows = wraw.shape
    chips = row_shards // cores
    blocks_here = depth_rows // phases
    stack = cores * width
    col_share = cols // depths
    main = stack // (8 * depths) * 8
    per = 8 // depths
    me_f, me_d, me_r = lax.axis_index("frame"), lax.axis_index("depth"), lax.axis_index("row")
    me_y, me_c = me_r // cores, lax.rem(me_r, cores)
    other_f, other_y = 1 - me_f, 1 - me_y
    same = 1 - lax.rem(me_f + me_c, 2)
    core_dev = (me_f, me_d, me_y * cores + 1 - me_c)

    barrier = pltpu.get_barrier_semaphore()

    def greet(device):
        pl.semaphore_signal(barrier, inc=1, device_id=device, device_id_type=pl.DeviceIdType.MESH)

    for chip in range(chips):
        for core in range(cores):
            to_chip, to_core = lax.rem(me_y + chip, chips), lax.rem(me_c + core, cores)
            device = (me_c, me_d, to_chip * cores + to_core)
            if chip or core:
                greet(device)
            else:
                pl.when(same == 0)(functools.partial(greet, device))
    pl.when(same == 0)(functools.partial(greet, core_dev))
    for step in range(1, depths):
        greet((me_f, lax.rem(me_d + step, depths), me_r))

    v_copy = pltpu.make_async_copy(v_hbm, raw, local_sem.at[0])
    v_copy.start()
    w_copy = pltpu.make_async_copy(w_hbm, wraw.at[me_c], local_sem.at[1])
    w_copy.start()
    region_copy = pltpu.make_async_copy(region_hbm, region, local_sem.at[2])
    region_copy.start()
    for part in range(2):
        slab[part, :depth_rows, :cols] = jnp.zeros((depth_rows, cols), jnp.bfloat16)
        slab[part, rows * depth_rows:, cols:] = jnp.zeros((depth_rows, cols), jnp.bfloat16)
    v_copy.wait()
    lanes_from_rows(raw, wide, pieces, vin)
    pl.semaphore_wait(barrier, frames * chips + depths - 1)

    def gather(part, index, device):
        return remote(vin.at[part], vol.at[part, me_r], g_send.at[part, index], g_recv.at[part, me_r], device)

    target = me_y * cores + me_f
    other_target = other_y * cores + me_f
    places = [(other_f, me_d, (chips - 1) * cores + me_f), (other_f, me_d, me_f), (me_f, me_d, other_target)]
    volume_copies = [[gather(part, index, place) for index, place in enumerate(places)] for part in range(2)]
    core_copies = [gather(part, len(places), core_dev) for part in range(2)]

    def start_part(part):
        for copy in volume_copies[part]:
            copy.start()
        pl.when(same == 0)(core_copies[part].start)

    start_part(0)

    @pl.when(same == 1)
    def _():
        for part in range(2):
            vol[part, me_r] = vin[part]

    for frame in range(frames):
        for chip in range(chips):
            device = (lax.rem(me_f + frame, frames), me_d, lax.rem(me_y + chip, chips) * cores + me_f)
            if frame or chip:
                pl.semaphore_signal(ready, inc=1, device_id=device, device_id_type=pl.DeviceIdType.MESH)
            else:
                @pl.when(same == 0)
                def _():
                    pl.semaphore_signal(ready, inc=1, device_id=device, device_id_type=pl.DeviceIdType.MESH)
    w_copy.wait()
    w_send = remote(wraw.at[me_c], wraw.at[me_c], p_send, p_recv, core_dev)
    w_send.start()
    region_copy.wait()
    w_send.wait_recv()
    start_part(1)
    for tap_col in range(TAP_SIDE):
        bands = []
        for at in range(TAP_SIDE):
            tap = (TAP_SIDE - 1 - at) * TAP_SIDE + tap_col
            bands.append(jnp.concatenate([wraw[core, tap].astype(jnp.float32) for core in range(cores)], axis=0))
        wflat[tap_col * stack:(tap_col + 1) * stack, :] = jnp.concatenate(bands, axis=1).astype(jnp.bfloat16)

    lane = lax.broadcasted_iota(jnp.int32, (1, cols), 1)
    place = lax.rem(lane, side)
    row8 = lax.broadcasted_iota(jnp.int32, (8, cols), 0)
    lane_block = lax.broadcasted_iota(jnp.int32, (8, cols), 1) // col_share
    first_block = me_f * blocks_here

    def take(part):
        for source in range(row_shards):
            def arrive():
                remote(vin.at[0], vol.at[part, source], g_send.at[part, 0], g_recv.at[part, source], core_dev).wait_recv()
            pl.when((same == 0) | (source != me_r))(arrive)
        ids = region[...]
        crossed = pltpu.roll(ids, side, 1)
        ahead = pltpu.roll(crossed, rows - 1, 0)
        ahead = jnp.where(row8 < rows - 1, ahead, -1)
        low = lane < side
        owners = [jnp.where(low, ahead, ids) if part else jnp.where(low, ids, ahead)][0]
        before = jnp.where(low, crossed[:1], -1) if part else jnp.where(low, -1, crossed[:1])
        def fill(start, stop):
            for at in range(start, stop):
                slot = at // rows_here
                if at % rows_here == 0:
                    data = vol[part, slot]
                else:
                    prior, later = max(slot, 0), min(slot + 1, row_shards - 1)
                    if part:
                        data = jnp.concatenate([vol[part, later][:, side:], vol[part, prior][:, :side]], axis=1)
                    else:
                        data = jnp.concatenate([vol[part, prior][:, side:], vol[part, later][:, :side]], axis=1)
                owner = before if at < 0 else owners[at:at + 1]
                for block in range(blocks_here):
                    keep = (owner == first_block + block).astype(jnp.float32).astype(jnp.bfloat16)
                    kept = data * keep
                    if at + reach <= rows:
                        top = (at + reach) * depth_rows + block * phases
                        slab[part, top:top + phases, :cols] = kept
                    if at >= 0:
                        top = at * depth_rows + block * phases
                        slab[part, top:top + phases, cols:] = kept

        fill(-1, rows // 2 + 1)
        return functools.partial(fill, rows // 2 + 1, rows)


    def multiply(part, group):
        top = group * rows // 2 * depth_rows
        cut = round_up(wflat.shape[0] // 2, 16)
        for low, high in ((0, cut), (cut, wflat.shape[0])):
            products[part, group, low:high, :] = jnp.dot(
                wflat[low:high, :], slab[part, top:top + TAP_SIDE * depth_rows, :], preferred_element_type=jnp.float32)

    def piece(part, pair, tap_col):
        left = pair % 2 * cols
        return products[part, pair // 2, tap_col * stack:(tap_col + 1) * stack, left:left + cols]

    def turn(value, shift):
        return pltpu.roll(value, shift % cols, 1)

    def emit(pair, total, shares):
        swapped = turn(total, side)
        upper, lower = (swapped, total) if shares[0] * col_share >= side else (total, swapped)
        peak = jnp.max(jnp.maximum(jnp.abs(upper), jnp.abs(lower)), axis=0, keepdims=True)
        code = jnp.ceil(8.0 * jnp.log2(jnp.maximum(peak, 1e-32)))
        inverse = LIMIT / jnp.exp2(code * 0.125)
        words = (jnp.round(upper * inverse).astype(jnp.int32) << 16) + jnp.round(lower * inverse).astype(jnp.int32)
        code = code.astype(jnp.int32)
        rest = words[depths * main:]
        for share in shares:
            start = share * col_share % side
            tile, extra = None, None
            for block in range(depths):
                shift = block * col_share - start
                moved = turn(words[block * main:(block + 1) * main], shift) if shift else words[block * main:(block + 1) * main]
                left = turn(rest, shift) if shift else rest
                tile = moved if tile is None else jnp.where(lane >= block * col_share, moved, tile)
                extra = left if extra is None else jnp.where(lane >= block * col_share, left, extra)
            extra = jnp.where(row8 // per == lane_block, extra, 0)
            step = 4
            while step >= per:
                extra = extra + pltpu.roll(extra, step, 0)
                step //= 2
            mark = jnp.where((lane >= start) & (lane < start + col_share), code, 0)
            mark = mark + turn(mark, cols // 2)
            mark = mark + turn(mark, cols // 4)
            outbox[pair, share, :main] = tile
            outbox[pair, share, main:main + per] = extra[:per]
            outbox[pair, share, main + per:] = mark

    def pack_first(pair):
        total = None
        for tap_col in range(TAP_SIDE):
            shift = tap_col - reach
            term = piece(0, pair, tap_col)
            if shift > 0:
                term = turn(jnp.where(place < side - shift, term, 0.0), shift)
            if shift < 0:
                term = turn(jnp.where(place >= -shift, term, 0.0), shift)
            total = term if total is None else total + term
        sums[pair] = total
        emit(pair, total, (0,))

    def pack_second(pair):
        near, far = sums[pair], None
        for tap_col in range(TAP_SIDE):
            shift = tap_col - reach
            term = piece(1, pair, tap_col)
            if shift > 0:
                term = turn(jnp.where(place < side - shift, term, piece(0, pair, tap_col)), shift)
            if shift < 0:
                near = near + turn(jnp.where(place < -shift, term, 0.0), shift)
                term = turn(jnp.where(place < -shift, 0.0, term), shift)
            far = term if far is None else far + term
        emit(pair, near, (1,))
        emit(pair, far, (2, 3))

    def message(index, share, pair, device_d):
        return remote(outbox.at[index, share], inbox.at[me_y, me_f, me_d], m_send.at[index, share],
                      m_recv.at[me_y, me_f, me_d], (me_c, device_d, pair))

    def each_message(pairs, shares, act, stay=None):
        for share in shares:
            for pair in pairs:
                copy = message(pair, share, pair, share)
                own = same * (me_r == pair).astype(jnp.int32) * (me_d == share).astype(jnp.int32)
                pl.when(own == 0)(functools.partial(act, copy))
                if stay is not None:
                    pl.when(own == 1)(functools.partial(stay, pair, share))

    def keep_own(pair, share):
        inbox[me_y, me_f, me_d] = outbox[pair, share]

    def send(pairs, shares):
        each_message(pairs, shares, lambda copy: copy.start(), keep_own)

    pl.semaphore_wait(ready, row_shards - same)
    fill = take(0)
    multiply(0, 0)
    pack_first(0)
    pack_first(1)
    send((0, 1), (0,))
    fill()
    multiply(0, 1)
    pack_first(2)
    pack_first(3)
    send((2, 3), (0,))
    fill = take(1)
    multiply(1, 0)
    fill()
    multiply(1, 1)
    pack_second(0)
    pack_second(1)
    send((0, 1), (3, 1, 2))
    pack_second(2)
    pack_second(3)
    send((2, 3), (3, 1, 2))
    received = [[None] * rows_here for _ in range(chips)]
    for frame_step in range(frames):
        frame = lax.rem(me_f + frame_step, frames)
        for step in range(depths):
            for chip in range(chips):
                depth = lax.rem(me_d + step, depths)

                def arrive():
                    remote(outbox.at[0, 0], inbox.at[chip, frame, depth], m_send.at[0, 0],
                           m_recv.at[chip, frame, depth], core_dev).wait_recv()
                if frame_step or step:
                    arrive()
                else:
                    pl.when((same == 0) | (chip != me_y))(arrive)
                block = inbox[chip, frame, depth]
                scale = jnp.exp2(block[main + per:].astype(jnp.float32) * 0.125) * (1.0 / LIMIT)
                lower = (block << 16) >> 16
                upper = ((block - lower) >> 16).astype(jnp.float32) * scale
                lower = lower.astype(jnp.float32) * scale
                received[chip] = [
                    term if held is None else held + term for held, term in zip(received[chip], (upper, lower))]
    halves = []
    for total in received:
        extra_rows = []
        for block in range(depths):
            moved = []
            for row in range(rows_here):
                shift = (row - block) * col_share % cols
                moved.append(pltpu.roll(total[row], shift, 1) if shift else total[row])
            merged = jnp.where(lane < col_share, moved[0], moved[1])
            halves.append(merged[:main])
            extra_rows.append(merged[main:main + per])
        halves.append(jnp.concatenate(extra_rows, axis=0))
    lanes_here = rows_here * col_share
    turned = jnp.concatenate(halves, axis=0).T[:lanes_here]
    group = math.lcm(phases, 128) // phases
    span = group * phases
    per_row = col_share // group
    members = []
    for half in range(pieces.shape[0]):
        count = min(128, phases - half * 128)
        pieces[half, :lanes_here, :count] = turned[:, half * 128:half * 128 + count]
    for member in range(group):
        for half in range(pieces.shape[0]):
            count = min(128, phases - half * 128)
            members.append(pieces[half, pl.ds(member, rows_here * per_row, stride=group), :][:, :count])
    strips = jnp.concatenate(members, axis=1)
    for row in range(rows_here):
        for at in range(per_row):
            line = row * per_row + at
            cam[row:row + 1, at * span:(at + 1) * span] = strips[line:line + 1]
    for part in range(2):
        for copy in volume_copies[part]:
            copy.wait_send()
        pl.when(same == 0)(core_copies[part].wait_send)
    w_send.wait_send()
    each_message(range(row_shards), range(depths), lambda copy: copy.wait_send())


def hand_over(camera_in, recorded, weight, camera_out, residual_out):
    camera_out[...] = camera_in[...]
    residual_out[...] = weight[...].astype(jnp.float32) * (camera_in[...] - recorded[...].astype(jnp.float32))


def fused_body(sizes, volume, point_spread, region_map, measured, pixel_weight):
    frames, depths, row_shards = sizes
    _, _, rows_here, merged = volume.shape
    cols = merged // PHASES
    _, depth_rows, taps, width = point_spread.shape
    rows = rows_here * row_shards
    stack = CORES * width
    lines = stack // depths + 1
    group = math.lcm(PHASES, 128) // PHASES
    span = group * PHASES
    image = (rows_here, cols // depths * PHASES)
    spread = point_spread.reshape(depth_rows, taps, width).transpose(1, 2, 0)
    vmem = pl.BlockSpec(memory_space=pltpu.VMEM)
    hbm = pl.BlockSpec(memory_space=pltpu.HBM)
    dma = pltpu.SemaphoreType.DMA
    camera = pl.pallas_call(
        functools.partial(kernel, frames, depths, row_shards),
        out_shape=jax.ShapeDtypeStruct(image, jnp.float32),
        in_specs=[hbm, hbm, hbm],
        out_specs=vmem,
        scratch_shapes=[
            pltpu.VMEM((rows_here, merged), jnp.bfloat16),
            pltpu.VMEM((rows_here * cols // group, span + 128), jnp.float32),
            pltpu.VMEM((round_up(PHASES, 128) // 128, rows_here * cols, 128), jnp.float32),
            pltpu.VMEM((2, PHASES, cols), jnp.bfloat16),
            pltpu.VMEM(region_map.shape, jnp.int32),
            pltpu.VMEM((2, row_shards, PHASES, cols), jnp.bfloat16),
            pltpu.VMEM((CORES, taps, width, depth_rows), jnp.bfloat16),
            pltpu.VMEM((TAP_SIDE * stack, TAP_SIDE * depth_rows), jnp.bfloat16),
            pltpu.VMEM((2, (rows + 1) * depth_rows, rows_here * cols), jnp.bfloat16),
            pltpu.VMEM((2, 2, TAP_SIDE * stack, rows_here * cols), jnp.float32),
            pltpu.VMEM((row_shards, stack, cols), jnp.float32),
            pltpu.VMEM((row_shards, depths, lines, cols), jnp.int32),
            pltpu.VMEM((row_shards // CORES, frames, depths, lines, cols), jnp.int32),
            pltpu.SemaphoreType.REGULAR, dma((3,)), dma((2, 4)), dma((2, row_shards)), dma, dma, dma((row_shards, depths)),
            dma((row_shards // CORES, frames, depths)),
        ],
        compiler_params=pltpu.CompilerParams(collective_id=0, has_side_effects=True, vmem_limit_bytes=24 << 20),
    )(*[pltpu.with_memory_space_constraint(each, pltpu.HBM) for each in (volume.reshape(rows_here, merged), spread, region_map)])
    camera, residual = pl.pallas_call(
        hand_over,
        out_shape=[jax.ShapeDtypeStruct(image, jnp.float32)] * 2,
        in_specs=[vmem] * 3,
        out_specs=[vmem, vmem],
        compiler_params=pltpu.CompilerParams(vmem_limit_bytes=4 << 20),
    )(camera, measured.reshape(image), pixel_weight.reshape(image))
    return (camera.reshape(measured.shape), residual.reshape(measured.shape))


def solution(mesh):
    in_specs = (
        P("depth", "frame", "row", None),
        P("depth", "frame", None, "row"),
        P(),
        P("frame", "row", "depth"),
        P("frame", "row", "depth"),
    )
    out_specs = (P("frame", "row", "depth"), P("frame", "row", "depth"))
    sizes = (mesh.shape["frame"], mesh.shape["depth"], mesh.shape["row"])

    def body(volume, *rest):
        blocks_fit = rest[0].shape[1] % PHASES == 0
        stack = CORES * rest[0].shape[3]
        packs = sizes[1] == 4 and stack % 8 == 0 and stack // 8 % sizes[1] == 1
        pairs = volume.shape[2] == 2 and (volume.shape[3] // PHASES) == 128
        if sizes[0] == 2 and sizes[2] == 2 * CORES and volume.shape[1] == 1 and blocks_fit and packs and pairs:
            return fused_body(sizes, volume, *rest)
        return plain_body(volume, *rest)

    return jax.shard_map(body, mesh=mesh, in_specs=in_specs, out_specs=out_specs, check_vma=False)
```

```python
import functools
import math

import jax
import jax.numpy as jnp
from jax import lax
from jax.experimental import pallas as pl
from jax.experimental.pallas import tpu as pltpu
from jax.sharding import PartitionSpec as P

PHASES = 144
BLOCKS = 4
TAP_SIDE = 5
CORES = 2
LIMIT = 32000.0


def build_taps(planes, region_rows):
    tap_reach = TAP_SIDE // 2
    frames, row_count, merged = planes.shape
    col_count = merged // PHASES
    split_planes = planes.reshape(frames, row_count, col_count, PHASES)
    block_ids = jnp.arange(BLOCKS, dtype=jnp.int32)
    onehot = (region_rows[:, :, None] == block_ids[None, None, :]).astype(jnp.bfloat16)
    expanded = (split_planes[:, :, :, None, :] * onehot[None, :, :, :, None]).reshape(
        frames, row_count, col_count, BLOCKS * PHASES
    )
    return jnp.pad(expanded, ((0, 0), (0, 0), (tap_reach, tap_reach), (0, 0)))


def project(padded, spread_local, out_rows):
    tap_reach = TAP_SIDE // 2
    frames, ext_rows, ext_cols, _ = padded.shape
    col_count = ext_cols - 2 * tap_reach
    out_width = spread_local.shape[2]
    zero_start = jnp.zeros((frames * out_rows * col_count, out_width), jnp.float32)
    running = zero_start
    spread_slab = lax.all_gather(spread_local, "frame", axis=0, tiled=True)
    piece_rows = spread_slab.shape[0]
    flat_cols = padded.reshape(frames * ext_rows * ext_cols, piece_rows)
    for tap_row in range(TAP_SIDE):
        row_taps = spread_slab[:, tap_row * TAP_SIDE : (tap_row + 1) * TAP_SIDE, :].reshape(
            piece_rows, TAP_SIDE * out_width
        )
        product = jnp.dot(flat_cols, row_taps, preferred_element_type=jnp.float32)
        product = product.reshape(frames, ext_rows, ext_cols, TAP_SIDE, out_width)
        first_row = 2 * tap_reach - tap_row
        for tap_col in range(TAP_SIDE):
            first_col = 2 * tap_reach - tap_col
            shifted = product[
                :, first_row : first_row + out_rows, first_col : first_col + col_count, tap_col, :
            ]
            running = running + shifted.reshape(frames * out_rows * col_count, out_width)
    partial_value = running.reshape(frames, out_rows, col_count * out_width)
    return lax.psum_scatter(partial_value, "depth", scatter_dimension=2, tiled=True)


def plain_body(volume, point_spread, region_map, measured, pixel_weight):
    tap_reach = TAP_SIDE // 2
    planes = volume[0]
    row_count = planes.shape[1]
    region_padded = jnp.pad(region_map, ((tap_reach, tap_reach), (0, 0)), constant_values=-1)
    all_rows = lax.all_gather(planes, "row", axis=1, tiled=True)
    extended = jnp.pad(all_rows, ((0, 0), (tap_reach, tap_reach), (0, 0)))
    padded = build_taps(extended, region_padded)
    piece_width = point_spread.shape[3]
    partial_value = project(padded, point_spread[0], all_rows.shape[1])
    frames, total_rows, merged = partial_value.shape
    split_partial = partial_value.reshape(frames, total_rows, merged // piece_width, piece_width)
    returned = lax.all_to_all(split_partial, "row", split_axis=1, concat_axis=3, tiled=True)
    camera = returned.reshape(frames, row_count, returned.shape[2] * returned.shape[3])
    residual = pixel_weight.astype(jnp.float32) * (camera - measured.astype(jnp.float32))
    return (camera, residual)


def round_up(value, step):
    return (value + step - 1) // step * step


def remote(src, dst, send_sem, recv_sem, device):
    return pltpu.make_async_remote_copy(
        src_ref=src, dst_ref=dst, send_sem=send_sem, recv_sem=recv_sem,
        device_id=device, device_id_type=pl.DeviceIdType.MESH,
    )


def lanes_from_rows(raw, wide, pieces, vin):
    _, phases, cols = vin.shape
    rows_here = raw.shape[0]
    group = math.lcm(phases, 128) // phases
    span = group * phases
    groups = cols // group
    wide[:, span:] = jnp.zeros((wide.shape[0], wide.shape[1] - span), jnp.float32)
    for at in range(groups):
        strip = raw[:, at * span:(at + 1) * span].astype(jnp.float32)
        for row in range(rows_here):
            wide[row * groups + at:row * groups + at + 1, :span] = strip[row:row + 1]
    for member in range(group):
        for half in range(pieces.shape[0]):
            first = member * phases + half * 128
            pieces[half, pl.ds(member, rows_here * groups, stride=group), :] = wide[:, first:first + 128]
    side = cols // 2
    for part in range(2):
        for half in range(pieces.shape[0]):
            count = min(128, phases - half * 128)
            rows = [pieces[half, row * cols + part * side:row * cols + (part + 1) * side, :] for row in range(rows_here)]
            turned = jnp.concatenate(rows[::-1] if part else rows, axis=0).T
            vin[part, half * 128:half * 128 + count, :] = turned[:count].astype(jnp.bfloat16)


def kernel(frames, depths, row_shards, v_hbm, w_hbm, region_hbm, cam, raw, wide, pieces, vin, region, vol, wraw,
           wflat, slab, products, sums, outbox, inbox, ready, local_sem, g_send, g_recv, p_send, p_recv, m_send, m_recv):
    reach = TAP_SIDE // 2
    _, phases, cols = vin.shape
    rows_here = raw.shape[0]
    side = cols // 2
    rows = rows_here * row_shards
    cores, taps, width, depth_rows = wraw.shape
    chips = row_shards // cores
    blocks_here = depth_rows // phases
    stack = cores * width
    col_share = cols // depths
    main = stack // (8 * depths) * 8
    per = 8 // depths
    me_f, me_d, me_r = lax.axis_index("frame"), lax.axis_index("depth"), lax.axis_index("row")
    me_y, me_c = me_r // cores, lax.rem(me_r, cores)
    other_f, other_y = 1 - me_f, 1 - me_y
    same = 1 - lax.rem(me_f + me_c, 2)
    core_dev = (me_f, me_d, me_y * cores + 1 - me_c)

    barrier = pltpu.get_barrier_semaphore()

    def greet(device):
        pl.semaphore_signal(barrier, inc=1, device_id=device, device_id_type=pl.DeviceIdType.MESH)

    for chip in range(chips):
        for core in range(cores):
            to_chip, to_core = lax.rem(me_y + chip, chips), lax.rem(me_c + core, cores)
            device = (me_c, me_d, to_chip * cores + to_core)
            if chip or core:
                greet(device)
            else:
                pl.when(same == 0)(functools.partial(greet, device))
    pl.when(same == 0)(functools.partial(greet, core_dev))
    for step in range(1, depths):
        greet((me_f, lax.rem(me_d + step, depths), me_r))

    v_copy = pltpu.make_async_copy(v_hbm, raw, local_sem.at[0])
    v_copy.start()
    w_copy = pltpu.make_async_copy(w_hbm, wraw.at[me_c], local_sem.at[1])
    w_copy.start()
    region_copy = pltpu.make_async_copy(region_hbm, region, local_sem.at[2])
    region_copy.start()
    for part in range(2):
        slab[part, :depth_rows, :cols] = jnp.zeros((depth_rows, cols), jnp.bfloat16)
        slab[part, rows * depth_rows:, cols:] = jnp.zeros((depth_rows, cols), jnp.bfloat16)
    v_copy.wait()
    lanes_from_rows(raw, wide, pieces, vin)
    pl.semaphore_wait(barrier, frames * chips + depths - 1)

    def gather(part, index, device):
        return remote(vin.at[part], vol.at[part, me_r], g_send.at[part, index], g_recv.at[part, me_r], device)

    target = me_y * cores + me_f
    other_target = other_y * cores + me_f
    places = [(other_f, me_d, (chips - 1) * cores + me_f), (other_f, me_d, me_f), (me_f, me_d, other_target)]
    volume_copies = [[gather(part, index, place) for index, place in enumerate(places)] for part in range(2)]
    core_copies = [gather(part, len(places), core_dev) for part in range(2)]

    def start_part(part):
        for copy in volume_copies[part]:
            copy.start()
        pl.when(same == 0)(core_copies[part].start)

    start_part(0)

    @pl.when(same == 1)
    def _():
        for part in range(2):
            vol[part, me_r] = vin[part]

    for frame in range(frames):
        for chip in range(chips):
            device = (lax.rem(me_f + frame, frames), me_d, lax.rem(me_y + chip, chips) * cores + me_f)
            if frame or chip:
                pl.semaphore_signal(ready, inc=1, device_id=device, device_id_type=pl.DeviceIdType.MESH)
            else:
                @pl.when(same == 0)
                def _():
                    pl.semaphore_signal(ready, inc=1, device_id=device, device_id_type=pl.DeviceIdType.MESH)
    w_copy.wait()
    w_send = remote(wraw.at[me_c], wraw.at[me_c], p_send, p_recv, core_dev)
    w_send.start()
    region_copy.wait()
    w_send.wait_recv()
    start_part(1)
    for tap_col in range(TAP_SIDE):
        bands = []
        for at in range(TAP_SIDE):
            tap = (TAP_SIDE - 1 - at) * TAP_SIDE + tap_col
            bands.append(jnp.concatenate([wraw[core, tap].astype(jnp.float32) for core in range(cores)], axis=0))
        wflat[tap_col * stack:(tap_col + 1) * stack, :] = jnp.concatenate(bands, axis=1).astype(jnp.bfloat16)

    lane = lax.broadcasted_iota(jnp.int32, (1, cols), 1)
    place = lax.rem(lane, side)
    row8 = lax.broadcasted_iota(jnp.int32, (8, cols), 0)
    lane_block = lax.broadcasted_iota(jnp.int32, (8, cols), 1) // col_share
    first_block = me_f * blocks_here

    def take(part):
        for source in range(row_shards):
            def arrive():
                remote(vin.at[0], vol.at[part, source], g_send.at[part, 0], g_recv.at[part, source], core_dev).wait_recv()
            pl.when((same == 0) | (source != me_r))(arrive)
        ids = region[...]
        crossed = pltpu.roll(ids, side, 1)
        ahead = pltpu.roll(crossed, rows - 1, 0)
        ahead = jnp.where(row8 < rows - 1, ahead, -1)
        low = lane < side
        owners = [jnp.where(low, ahead, ids) if part else jnp.where(low, ids, ahead)][0]
        before = jnp.where(low, crossed[:1], -1) if part else jnp.where(low, -1, crossed[:1])
        for at in range(-1, rows):
            slot = at // rows_here
            if at % rows_here == 0:
                data = vol[part, slot]
            else:
                prior, later = max(slot, 0), min(slot + 1, row_shards - 1)
                if part:
                    data = jnp.concatenate([vol[part, later][:, side:], vol[part, prior][:, :side]], axis=1)
                else:
                    data = jnp.concatenate([vol[part, prior][:, side:], vol[part, later][:, :side]], axis=1)
            owner = before if at < 0 else owners[at:at + 1]
            for block in range(blocks_here):
                keep = (owner == first_block + block).astype(jnp.float32).astype(jnp.bfloat16)
                kept = data * keep
                if at + reach <= rows:
                    top = (at + reach) * depth_rows + block * phases
                    slab[part, top:top + phases, :cols] = kept
                if at >= 0:
                    top = at * depth_rows + block * phases
                    slab[part, top:top + phases, cols:] = kept

    def multiply(part, group):
        top = group * rows // 2 * depth_rows
        cut = round_up(wflat.shape[0] // 2, 16)
        for low, high in ((0, cut), (cut, wflat.shape[0])):
            products[part, group, low:high, :] = jnp.dot(
                wflat[low:high, :], slab[part, top:top + TAP_SIDE * depth_rows, :], preferred_element_type=jnp.float32)

    def piece(part, pair, tap_col):
        left = pair % 2 * cols
        return products[part, pair // 2, tap_col * stack:(tap_col + 1) * stack, left:left + cols]

    def turn(value, shift):
        return pltpu.roll(value, shift % cols, 1)

    def emit(pair, total, shares):
        swapped = turn(total, side)
        upper, lower = (swapped, total) if shares[0] * col_share >= side else (total, swapped)
        peak = jnp.max(jnp.maximum(jnp.abs(upper), jnp.abs(lower)), axis=0, keepdims=True)
        code = jnp.ceil(8.0 * jnp.log2(jnp.maximum(peak, 1e-32)))
        inverse = LIMIT / jnp.exp2(code * 0.125)
        words = (jnp.round(upper * inverse).astype(jnp.int32) << 16) + jnp.round(lower * inverse).astype(jnp.int32)
        code = code.astype(jnp.int32)
        rest = words[depths * main:]
        for share in shares:
            start = share * col_share % side
            tile, extra = None, None
            for block in range(depths):
                shift = block * col_share - start
                moved = turn(words[block * main:(block + 1) * main], shift) if shift else words[block * main:(block + 1) * main]
                left = turn(rest, shift) if shift else rest
                tile = moved if tile is None else jnp.where(lane >= block * col_share, moved, tile)
                extra = left if extra is None else jnp.where(lane >= block * col_share, left, extra)
            extra = jnp.where(row8 // per == lane_block, extra, 0)
            step = 4
            while step >= per:
                extra = extra + pltpu.roll(extra, step, 0)
                step //= 2
            mark = jnp.where((lane >= start) & (lane < start + col_share), code, 0)
            mark = mark + turn(mark, cols // 2)
            mark = mark + turn(mark, cols // 4)
            outbox[pair, share, :main] = tile
            outbox[pair, share, main:main + per] = extra[:per]
            outbox[pair, share, main + per:] = mark

    def pack_first(pair):
        total = None
        for tap_col in range(TAP_SIDE):
            shift = tap_col - reach
            term = piece(0, pair, tap_col)
            if shift > 0:
                term = turn(jnp.where(place < side - shift, term, 0.0), shift)
            if shift < 0:
                term = turn(jnp.where(place >= -shift, term, 0.0), shift)
            total = term if total is None else total + term
        sums[pair] = total
        emit(pair, total, (0,))

    def pack_second(pair):
        near, far = sums[pair], None
        for tap_col in range(TAP_SIDE):
            shift = tap_col - reach
            term = piece(1, pair, tap_col)
            if shift > 0:
                term = turn(jnp.where(place < side - shift, term, piece(0, pair, tap_col)), shift)
            if shift < 0:
                near = near + turn(jnp.where(place < -shift, term, 0.0), shift)
                term = turn(jnp.where(place < -shift, 0.0, term), shift)
            far = term if far is None else far + term
        emit(pair, near, (1,))
        emit(pair, far, (2, 3))

    def message(index, share, pair, device_d):
        return remote(outbox.at[index, share], inbox.at[me_y, me_f, me_d], m_send.at[index, share],
                      m_recv.at[me_y, me_f, me_d], (me_c, device_d, pair))

    def each_message(pairs, shares, act, stay=None):
        for share in shares:
            for pair in pairs:
                copy = message(pair, share, pair, share)
                own = same * (me_r == pair).astype(jnp.int32) * (me_d == share).astype(jnp.int32)
                pl.when(own == 0)(functools.partial(act, copy))
                if stay is not None:
                    pl.when(own == 1)(functools.partial(stay, pair, share))

    def keep_own(pair, share):
        inbox[me_y, me_f, me_d] = outbox[pair, share]

    def send(pairs, shares):
        each_message(pairs, shares, lambda copy: copy.start(), keep_own)

    pl.semaphore_wait(ready, row_shards - same)
    take(0)
    multiply(0, 0)
    pack_first(0)
    send((0,), (0,))
    pack_first(1)
    send((1,), (0,))
    multiply(0, 1)
    pack_first(2)
    pack_first(3)
    send((2, 3), (0,))
    take(1)
    multiply(1, 0)
    multiply(1, 1)
    pack_second(0)
    pack_second(1)
    send((0, 1), range(1, depths))
    pack_second(2)
    pack_second(3)
    send((2, 3), range(1, depths))
    received = [[None] * rows_here for _ in range(chips)]
    for frame_step in range(frames):
        frame = lax.rem(me_f + frame_step, frames)
        for step in range(depths):
            for chip in range(chips):
                depth = lax.rem(me_d + step, depths)

                def arrive():
                    remote(outbox.at[0, 0], inbox.at[chip, frame, depth], m_send.at[0, 0],
                           m_recv.at[chip, frame, depth], core_dev).wait_recv()
                if frame_step or step:
                    arrive()
                else:
                    pl.when((same == 0) | (chip != me_y))(arrive)
                block = inbox[chip, frame, depth]
                scale = jnp.exp2(block[main + per:].astype(jnp.float32) * 0.125) * (1.0 / LIMIT)
                lower = (block << 16) >> 16
                upper = ((block - lower) >> 16).astype(jnp.float32) * scale
                lower = lower.astype(jnp.float32) * scale
                received[chip] = [
                    term if held is None else held + term for held, term in zip(received[chip], (upper, lower))]
    halves = []
    for total in received:
        extra_rows = []
        for block in range(depths):
            moved = []
            for row in range(rows_here):
                shift = (row - block) * col_share % cols
                moved.append(pltpu.roll(total[row], shift, 1) if shift else total[row])
            merged = jnp.where(lane < col_share, moved[0], moved[1])
            halves.append(merged[:main])
            extra_rows.append(merged[main:main + per])
        halves.append(jnp.concatenate(extra_rows, axis=0))
    lanes_here = rows_here * col_share
    turned = jnp.concatenate(halves, axis=0).T[:lanes_here]
    group = math.lcm(phases, 128) // phases
    span = group * phases
    per_row = col_share // group
    members = []
    for half in range(pieces.shape[0]):
        count = min(128, phases - half * 128)
        pieces[half, :lanes_here, :count] = turned[:, half * 128:half * 128 + count]
    for member in range(group):
        for half in range(pieces.shape[0]):
            count = min(128, phases - half * 128)
            members.append(pieces[half, pl.ds(member, rows_here * per_row, stride=group), :][:, :count])
    strips = jnp.concatenate(members, axis=1)
    for row in range(rows_here):
        for at in range(per_row):
            line = row * per_row + at
            cam[row:row + 1, at * span:(at + 1) * span] = strips[line:line + 1]
    for part in range(2):
        for copy in volume_copies[part]:
            copy.wait_send()
        pl.when(same == 0)(core_copies[part].wait_send)
    w_send.wait_send()
    each_message(range(row_shards), range(depths), lambda copy: copy.wait_send())


def hand_over(camera_in, recorded, weight, camera_out, residual_out):
    camera_out[...] = camera_in[...]
    residual_out[...] = weight[...].astype(jnp.float32) * (camera_in[...] - recorded[...].astype(jnp.float32))


def fused_body(sizes, volume, point_spread, region_map, measured, pixel_weight):
    frames, depths, row_shards = sizes
    _, _, rows_here, merged = volume.shape
    cols = merged // PHASES
    _, depth_rows, taps, width = point_spread.shape
    rows = rows_here * row_shards
    stack = CORES * width
    lines = stack // depths + 1
    group = math.lcm(PHASES, 128) // PHASES
    span = group * PHASES
    image = (rows_here, cols // depths * PHASES)
    spread = point_spread.reshape(depth_rows, taps, width).transpose(1, 2, 0)
    vmem = pl.BlockSpec(memory_space=pltpu.VMEM)
    hbm = pl.BlockSpec(memory_space=pltpu.HBM)
    dma = pltpu.SemaphoreType.DMA
    camera = pl.pallas_call(
        functools.partial(kernel, frames, depths, row_shards),
        out_shape=jax.ShapeDtypeStruct(image, jnp.float32),
        in_specs=[hbm, hbm, hbm],
        out_specs=vmem,
        scratch_shapes=[
            pltpu.VMEM((rows_here, merged), jnp.bfloat16),
            pltpu.VMEM((rows_here * cols // group, span + 128), jnp.float32),
            pltpu.VMEM((round_up(PHASES, 128) // 128, rows_here * cols, 128), jnp.float32),
            pltpu.VMEM((2, PHASES, cols), jnp.bfloat16),
            pltpu.VMEM(region_map.shape, jnp.int32),
            pltpu.VMEM((2, row_shards, PHASES, cols), jnp.bfloat16),
            pltpu.VMEM((CORES, taps, width, depth_rows), jnp.bfloat16),
            pltpu.VMEM((TAP_SIDE * stack, TAP_SIDE * depth_rows), jnp.bfloat16),
            pltpu.VMEM((2, (rows + 1) * depth_rows, rows_here * cols), jnp.bfloat16),
            pltpu.VMEM((2, 2, TAP_SIDE * stack, rows_here * cols), jnp.float32),
            pltpu.VMEM((row_shards, stack, cols), jnp.float32),
            pltpu.VMEM((row_shards, depths, lines, cols), jnp.int32),
            pltpu.VMEM((row_shards // CORES, frames, depths, lines, cols), jnp.int32),
            pltpu.SemaphoreType.REGULAR, dma((3,)), dma((2, 4)), dma((2, row_shards)), dma, dma, dma((row_shards, depths)),
            dma((row_shards // CORES, frames, depths)),
        ],
        compiler_params=pltpu.CompilerParams(collective_id=0, has_side_effects=True, vmem_limit_bytes=24 << 20),
    )(*[pltpu.with_memory_space_constraint(each, pltpu.HBM) for each in (volume.reshape(rows_here, merged), spread, region_map)])
    camera, residual = pl.pallas_call(
        hand_over,
        out_shape=[jax.ShapeDtypeStruct(image, jnp.float32)] * 2,
        in_specs=[vmem] * 3,
        out_specs=[vmem, vmem],
        compiler_params=pltpu.CompilerParams(vmem_limit_bytes=4 << 20),
    )(camera, measured.reshape(image), pixel_weight.reshape(image))
    return (camera.reshape(measured.shape), residual.reshape(measured.shape))


def solution(mesh):
    in_specs = (
        P("depth", "frame", "row", None),
        P("depth", "frame", None, "row"),
        P(),
        P("frame", "row", "depth"),
        P("frame", "row", "depth"),
    )
    out_specs = (P("frame", "row", "depth"), P("frame", "row", "depth"))
    sizes = (mesh.shape["frame"], mesh.shape["depth"], mesh.shape["row"])

    def body(volume, *rest):
        blocks_fit = rest[0].shape[1] % PHASES == 0
        stack = CORES * rest[0].shape[3]
        packs = sizes[1] == 4 and stack % 8 == 0 and stack // 8 % sizes[1] == 1
        pairs = volume.shape[2] == 2 and (volume.shape[3] // PHASES) == 128
        if sizes[0] == 2 and sizes[2] == 2 * CORES and volume.shape[1] == 1 and blocks_fit and packs and pairs:
            return fused_body(sizes, volume, *rest)
        return plain_body(volume, *rest)

    return jax.shard_map(body, mesh=mesh, in_specs=in_specs, out_specs=out_specs, check_vma=False)
```

```python
import functools
import math

import jax
import jax.numpy as jnp
from jax import lax
from jax.experimental import pallas as pl
from jax.experimental.pallas import tpu as pltpu
from jax.sharding import PartitionSpec as P

PHASES = 144
BLOCKS = 4
TAP_SIDE = 5
CORES = 2
LIMIT = 32000.0


def build_taps(planes, region_rows):
    tap_reach = TAP_SIDE // 2
    frames, row_count, merged = planes.shape
    col_count = merged // PHASES
    split_planes = planes.reshape(frames, row_count, col_count, PHASES)
    block_ids = jnp.arange(BLOCKS, dtype=jnp.int32)
    onehot = (region_rows[:, :, None] == block_ids[None, None, :]).astype(jnp.bfloat16)
    expanded = (split_planes[:, :, :, None, :] * onehot[None, :, :, :, None]).reshape(
        frames, row_count, col_count, BLOCKS * PHASES
    )
    return jnp.pad(expanded, ((0, 0), (0, 0), (tap_reach, tap_reach), (0, 0)))


def project(padded, spread_local, out_rows):
    tap_reach = TAP_SIDE // 2
    frames, ext_rows, ext_cols, _ = padded.shape
    col_count = ext_cols - 2 * tap_reach
    out_width = spread_local.shape[2]
    zero_start = jnp.zeros((frames * out_rows * col_count, out_width), jnp.float32)
    running = zero_start
    spread_slab = lax.all_gather(spread_local, "frame", axis=0, tiled=True)
    piece_rows = spread_slab.shape[0]
    flat_cols = padded.reshape(frames * ext_rows * ext_cols, piece_rows)
    for tap_row in range(TAP_SIDE):
        row_taps = spread_slab[:, tap_row * TAP_SIDE : (tap_row + 1) * TAP_SIDE, :].reshape(
            piece_rows, TAP_SIDE * out_width
        )
        product = jnp.dot(flat_cols, row_taps, preferred_element_type=jnp.float32)
        product = product.reshape(frames, ext_rows, ext_cols, TAP_SIDE, out_width)
        first_row = 2 * tap_reach - tap_row
        for tap_col in range(TAP_SIDE):
            first_col = 2 * tap_reach - tap_col
            shifted = product[
                :, first_row : first_row + out_rows, first_col : first_col + col_count, tap_col, :
            ]
            running = running + shifted.reshape(frames * out_rows * col_count, out_width)
    partial_value = running.reshape(frames, out_rows, col_count * out_width)
    return lax.psum_scatter(partial_value, "depth", scatter_dimension=2, tiled=True)


def plain_body(volume, point_spread, region_map, measured, pixel_weight):
    tap_reach = TAP_SIDE // 2
    planes = volume[0]
    row_count = planes.shape[1]
    region_padded = jnp.pad(region_map, ((tap_reach, tap_reach), (0, 0)), constant_values=-1)
    all_rows = lax.all_gather(planes, "row", axis=1, tiled=True)
    extended = jnp.pad(all_rows, ((0, 0), (tap_reach, tap_reach), (0, 0)))
    padded = build_taps(extended, region_padded)
    piece_width = point_spread.shape[3]
    partial_value = project(padded, point_spread[0], all_rows.shape[1])
    frames, total_rows, merged = partial_value.shape
    split_partial = partial_value.reshape(frames, total_rows, merged // piece_width, piece_width)
    returned = lax.all_to_all(split_partial, "row", split_axis=1, concat_axis=3, tiled=True)
    camera = returned.reshape(frames, row_count, returned.shape[2] * returned.shape[3])
    residual = pixel_weight.astype(jnp.float32) * (camera - measured.astype(jnp.float32))
    return (camera, residual)


def round_up(value, step):
    return (value + step - 1) // step * step


def remote(src, dst, send_sem, recv_sem, device):
    return pltpu.make_async_remote_copy(
        src_ref=src, dst_ref=dst, send_sem=send_sem, recv_sem=recv_sem,
        device_id=device, device_id_type=pl.DeviceIdType.MESH,
    )


def lanes_from_rows(raw, wide, pieces, vin):
    _, phases, cols = vin.shape
    rows_here = raw.shape[0]
    group = math.lcm(phases, 128) // phases
    span = group * phases
    groups = cols // group
    wide[:, span:] = jnp.zeros((wide.shape[0], wide.shape[1] - span), jnp.float32)
    for at in range(groups):
        strip = raw[:, at * span:(at + 1) * span].astype(jnp.float32)
        for row in range(rows_here):
            wide[row * groups + at:row * groups + at + 1, :span] = strip[row:row + 1]
    for member in range(group):
        for half in range(pieces.shape[0]):
            first = member * phases + half * 128
            pieces[half, pl.ds(member, rows_here * groups, stride=group), :] = wide[:, first:first + 128]
    side = cols // 2
    for part in range(2):
        for half in range(pieces.shape[0]):
            count = min(128, phases - half * 128)
            rows = [pieces[half, row * cols + part * side:row * cols + (part + 1) * side, :] for row in range(rows_here)]
            turned = jnp.concatenate(rows[::-1] if part else rows, axis=0).T
            vin[part, half * 128:half * 128 + count, :] = turned[:count].astype(jnp.bfloat16)


def kernel(frames, depths, row_shards, v_hbm, w_hbm, region_hbm, cam, raw, wide, pieces, vin, region, vol, wraw,
           wflat, slab, products, sums, outbox, inbox, ready, local_sem, g_send, g_recv, p_send, p_recv, m_send, m_recv):
    reach = TAP_SIDE // 2
    _, phases, cols = vin.shape
    rows_here = raw.shape[0]
    side = cols // 2
    rows = rows_here * row_shards
    cores, taps, width, depth_rows = wraw.shape
    chips = row_shards // cores
    blocks_here = depth_rows // phases
    stack = cores * width
    col_share = cols // depths
    main = stack // (8 * depths) * 8
    per = 8 // depths
    me_f, me_d, me_r = lax.axis_index("frame"), lax.axis_index("depth"), lax.axis_index("row")
    me_y, me_c = me_r // cores, lax.rem(me_r, cores)
    other_f, other_y = 1 - me_f, 1 - me_y
    same = 1 - lax.rem(me_f + me_c, 2)
    core_dev = (me_f, me_d, me_y * cores + 1 - me_c)

    barrier = pltpu.get_barrier_semaphore()

    def greet(device):
        pl.semaphore_signal(barrier, inc=1, device_id=device, device_id_type=pl.DeviceIdType.MESH)

    for chip in range(chips):
        for core in range(cores):
            to_chip, to_core = lax.rem(me_y + chip, chips), lax.rem(me_c + core, cores)
            device = (me_c, me_d, to_chip * cores + to_core)
            if chip or core:
                greet(device)
            else:
                pl.when(same == 0)(functools.partial(greet, device))
    pl.when(same == 0)(functools.partial(greet, core_dev))
    for step in range(1, depths):
        greet((me_f, lax.rem(me_d + step, depths), me_r))

    v_copy = pltpu.make_async_copy(v_hbm, raw, local_sem.at[0])
    v_copy.start()
    w_copy = pltpu.make_async_copy(w_hbm, wraw.at[me_c], local_sem.at[1])
    w_copy.start()
    region_copy = pltpu.make_async_copy(region_hbm, region, local_sem.at[2])
    region_copy.start()
    for part in range(2):
        slab[part, :depth_rows, :cols] = jnp.zeros((depth_rows, cols), jnp.bfloat16)
        slab[part, rows * depth_rows:, cols:] = jnp.zeros((depth_rows, cols), jnp.bfloat16)
    v_copy.wait()
    lanes_from_rows(raw, wide, pieces, vin)
    pl.semaphore_wait(barrier, frames * chips + depths - 1)

    def gather(part, index, device):
        return remote(vin.at[part], vol.at[part, me_r], g_send.at[part, index], g_recv.at[part, me_r], device)

    target = me_y * cores + me_f
    other_target = other_y * cores + me_f
    places = [(other_f, me_d, (chips - 1) * cores + me_f), (other_f, me_d, me_f), (me_f, me_d, other_target)]
    volume_copies = [[gather(part, index, place) for index, place in enumerate(places)] for part in range(2)]
    core_copies = [gather(part, len(places), core_dev) for part in range(2)]

    def start_part(part):
        for copy in volume_copies[part]:
            copy.start()
        pl.when(same == 0)(core_copies[part].start)

    start_part(0)

    @pl.when(same == 1)
    def _():
        for part in range(2):
            vol[part, me_r] = vin[part]

    for frame in range(frames):
        for chip in range(chips):
            device = (lax.rem(me_f + frame, frames), me_d, lax.rem(me_y + chip, chips) * cores + me_f)
            if frame or chip:
                pl.semaphore_signal(ready, inc=1, device_id=device, device_id_type=pl.DeviceIdType.MESH)
            else:
                @pl.when(same == 0)
                def _():
                    pl.semaphore_signal(ready, inc=1, device_id=device, device_id_type=pl.DeviceIdType.MESH)
    w_copy.wait()
    w_send = remote(wraw.at[me_c], wraw.at[me_c], p_send, p_recv, core_dev)
    w_send.start()
    region_copy.wait()
    w_send.wait_recv()
    start_part(1)
    for tap_col in range(TAP_SIDE):
        bands = []
        for at in range(TAP_SIDE):
            tap = (TAP_SIDE - 1 - at) * TAP_SIDE + tap_col
            bands.append(jnp.concatenate([wraw[core, tap].astype(jnp.float32) for core in range(cores)], axis=0))
        wflat[tap_col * stack:(tap_col + 1) * stack, :] = jnp.concatenate(bands, axis=1).astype(jnp.bfloat16)

    lane = lax.broadcasted_iota(jnp.int32, (1, cols), 1)
    place = lax.rem(lane, side)
    row8 = lax.broadcasted_iota(jnp.int32, (8, cols), 0)
    lane_block = lax.broadcasted_iota(jnp.int32, (8, cols), 1) // col_share
    first_block = me_f * blocks_here

    def take(part):
        for source in range(row_shards):
            def arrive():
                remote(vin.at[0], vol.at[part, source], g_send.at[part, 0], g_recv.at[part, source], core_dev).wait_recv()
            pl.when((same == 0) | (source != me_r))(arrive)
        ids = region[...]
        crossed = pltpu.roll(ids, side, 1)
        ahead = pltpu.roll(crossed, rows - 1, 0)
        ahead = jnp.where(row8 < rows - 1, ahead, -1)
        low = lane < side
        owners = [jnp.where(low, ahead, ids) if part else jnp.where(low, ids, ahead)][0]
        before = jnp.where(low, crossed[:1], -1) if part else jnp.where(low, -1, crossed[:1])
        for at in range(-1, rows):
            slot = at // rows_here
            if at % rows_here == 0:
                data = vol[part, slot]
            else:
                prior, later = max(slot, 0), min(slot + 1, row_shards - 1)
                if part:
                    data = jnp.concatenate([vol[part, later][:, side:], vol[part, prior][:, :side]], axis=1)
                else:
                    data = jnp.concatenate([vol[part, prior][:, side:], vol[part, later][:, :side]], axis=1)
            owner = before if at < 0 else owners[at:at + 1]
            for block in range(blocks_here):
                keep = (owner == first_block + block).astype(jnp.float32).astype(jnp.bfloat16)
                kept = data * keep
                if at + reach <= rows:
                    top = (at + reach) * depth_rows + block * phases
                    slab[part, top:top + phases, :cols] = kept
                if at >= 0:
                    top = at * depth_rows + block * phases
                    slab[part, top:top + phases, cols:] = kept

    def multiply(part, group):
        top = group * rows // 2 * depth_rows
        cut = round_up(wflat.shape[0] // 2, 16)
        for low, high in ((0, cut), (cut, wflat.shape[0])):
            products[part, group, low:high, :] = jnp.dot(
                wflat[low:high, :], slab[part, top:top + TAP_SIDE * depth_rows, :], preferred_element_type=jnp.float32)

    def piece(part, pair, tap_col):
        left = pair % 2 * cols
        return products[part, pair // 2, tap_col * stack:(tap_col + 1) * stack, left:left + cols]

    def turn(value, shift):
        return pltpu.roll(value, shift % cols, 1)

    def emit(pair, total, shares):
        swapped = turn(total, side)
        upper, lower = (swapped, total) if shares[0] * col_share >= side else (total, swapped)
        peak = jnp.max(jnp.maximum(jnp.abs(upper), jnp.abs(lower)), axis=0, keepdims=True)
        code = jnp.ceil(8.0 * jnp.log2(jnp.maximum(peak, 1e-32)))
        inverse = LIMIT / jnp.exp2(code * 0.125)
        words = (jnp.round(upper * inverse).astype(jnp.int32) << 16) + jnp.round(lower * inverse).astype(jnp.int32)
        code = code.astype(jnp.int32)
        rest = words[depths * main:]
        for share in shares:
            start = share * col_share % side
            tile, extra = None, None
            for block in range(depths):
                shift = block * col_share - start
                moved = turn(words[block * main:(block + 1) * main], shift) if shift else words[block * main:(block + 1) * main]
                left = turn(rest, shift) if shift else rest
                tile = moved if tile is None else jnp.where(lane >= block * col_share, moved, tile)
                extra = left if extra is None else jnp.where(lane >= block * col_share, left, extra)
            extra = jnp.where(row8 // per == lane_block, extra, 0)
            step = 4
            while step >= per:
                extra = extra + pltpu.roll(extra, step, 0)
                step //= 2
            mark = jnp.where((lane >= start) & (lane < start + col_share), code, 0)
            mark = mark + turn(mark, cols // 2)
            mark = mark + turn(mark, cols // 4)
            outbox[pair, share, :main] = tile
            outbox[pair, share, main:main + per] = extra[:per]
            outbox[pair, share, main + per:] = mark

    def pack_first(pair):
        total = None
        for tap_col in range(TAP_SIDE):
            shift = tap_col - reach
            term = piece(0, pair, tap_col)
            if shift > 0:
                term = turn(jnp.where(place < side - shift, term, 0.0), shift)
            if shift < 0:
                term = turn(jnp.where(place >= -shift, term, 0.0), shift)
            total = term if total is None else total + term
        sums[pair] = total
        emit(pair, total, (0,))

    def pack_second(pair):
        near, far = sums[pair], None
        for tap_col in range(TAP_SIDE):
            shift = tap_col - reach
            term = piece(1, pair, tap_col)
            if shift > 0:
                term = turn(jnp.where(place < side - shift, term, piece(0, pair, tap_col)), shift)
            if shift < 0:
                near = near + turn(jnp.where(place < -shift, term, 0.0), shift)
                term = turn(jnp.where(place < -shift, 0.0, term), shift)
            far = term if far is None else far + term
        emit(pair, near, (1,))
        emit(pair, far, (2, 3))

    def message(index, share, pair, device_d):
        return remote(outbox.at[index, share], inbox.at[me_y, me_f, me_d], m_send.at[index, share],
                      m_recv.at[me_y, me_f, me_d], (me_c, device_d, pair))

    def each_message(pairs, shares, act, stay=None):
        for share in shares:
            for pair in pairs:
                copy = message(pair, share, pair, share)
                own = same * (me_r == pair).astype(jnp.int32) * (me_d == share).astype(jnp.int32)
                pl.when(own == 0)(functools.partial(act, copy))
                if stay is not None:
                    pl.when(own == 1)(functools.partial(stay, pair, share))

    def keep_own(pair, share):
        inbox[me_y, me_f, me_d] = outbox[pair, share]

    def send(pairs, shares):
        each_message(pairs, shares, lambda copy: copy.start(), keep_own)

    pl.semaphore_wait(ready, row_shards - same)
    take(0)
    multiply(0, 0)
    pack_first(0)
    pack_first(1)
    send((0, 1), (0,))
    multiply(0, 1)
    pack_first(2)
    pack_first(3)
    send((2, 3), (0,))
    take(1)
    multiply(1, 0)
    multiply(1, 1)
    pack_second(0)
    pack_second(1)
    send((0, 1), (3, 1, 2))
    pack_second(2)
    pack_second(3)
    send((2, 3), (3, 1, 2))
    received = [[None] * rows_here for _ in range(chips)]
    for frame_step in range(frames):
        frame = lax.rem(me_f + frame_step, frames)
        for step in range(depths):
            for chip in range(chips):
                depth = lax.rem(me_d + step, depths)

                def arrive():
                    remote(outbox.at[0, 0], inbox.at[chip, frame, depth], m_send.at[0, 0],
                           m_recv.at[chip, frame, depth], core_dev).wait_recv()
                if frame_step or step:
                    arrive()
                else:
                    pl.when((same == 0) | (chip != me_y))(arrive)
                block = inbox[chip, frame, depth]
                scale = jnp.exp2(block[main + per:].astype(jnp.float32) * 0.125) * (1.0 / LIMIT)
                lower = (block << 16) >> 16
                upper = (block - lower).astype(jnp.float32) * (scale * (1.0 / 65536.0))
                lower = lower.astype(jnp.float32) * scale
                received[chip] = [
                    term if held is None else held + term for held, term in zip(received[chip], (upper, lower))]
    halves = []
    for total in received:
        extra_rows = []
        for block in range(depths):
            moved = []
            for row in range(rows_here):
                shift = (row - block) * col_share % cols
                moved.append(pltpu.roll(total[row], shift, 1) if shift else total[row])
            merged = jnp.where(lane < col_share, moved[0], moved[1])
            halves.append(merged[:main])
            extra_rows.append(merged[main:main + per])
        halves.append(jnp.concatenate(extra_rows, axis=0))
    lanes_here = rows_here * col_share
    turned = jnp.concatenate(halves, axis=0).T[:lanes_here]
    group = math.lcm(phases, 128) // phases
    span = group * phases
    per_row = col_share // group
    members = []
    for half in range(pieces.shape[0]):
        count = min(128, phases - half * 128)
        pieces[half, :lanes_here, :count] = turned[:, half * 128:half * 128 + count]
    for member in range(group):
        for half in range(pieces.shape[0]):
            count = min(128, phases - half * 128)
            members.append(pieces[half, pl.ds(member, rows_here * per_row, stride=group), :][:, :count])
    strips = jnp.concatenate(members, axis=1)
    for row in range(rows_here):
        for at in range(per_row):
            line = row * per_row + at
            cam[row:row + 1, at * span:(at + 1) * span] = strips[line:line + 1]
    for part in range(2):
        for copy in volume_copies[part]:
            copy.wait_send()
        pl.when(same == 0)(core_copies[part].wait_send)
    w_send.wait_send()
    each_message(range(row_shards), range(depths), lambda copy: copy.wait_send())


def hand_over(camera_in, recorded, weight, camera_out, residual_out):
    camera_out[...] = camera_in[...]
    residual_out[...] = weight[...].astype(jnp.float32) * (camera_in[...] - recorded[...].astype(jnp.float32))


def fused_body(sizes, volume, point_spread, region_map, measured, pixel_weight):
    frames, depths, row_shards = sizes
    _, _, rows_here, merged = volume.shape
    cols = merged // PHASES
    _, depth_rows, taps, width = point_spread.shape
    rows = rows_here * row_shards
    stack = CORES * width
    lines = stack // depths + 1
    group = math.lcm(PHASES, 128) // PHASES
    span = group * PHASES
    image = (rows_here, cols // depths * PHASES)
    spread = point_spread.reshape(depth_rows, taps, width).transpose(1, 2, 0)
    vmem = pl.BlockSpec(memory_space=pltpu.VMEM)
    hbm = pl.BlockSpec(memory_space=pltpu.HBM)
    dma = pltpu.SemaphoreType.DMA
    camera = pl.pallas_call(
        functools.partial(kernel, frames, depths, row_shards),
        out_shape=jax.ShapeDtypeStruct(image, jnp.float32),
        in_specs=[hbm, hbm, hbm],
        out_specs=vmem,
        scratch_shapes=[
            pltpu.VMEM((rows_here, merged), jnp.bfloat16),
            pltpu.VMEM((rows_here * cols // group, span + 128), jnp.float32),
            pltpu.VMEM((round_up(PHASES, 128) // 128, rows_here * cols, 128), jnp.float32),
            pltpu.VMEM((2, PHASES, cols), jnp.bfloat16),
            pltpu.VMEM(region_map.shape, jnp.int32),
            pltpu.VMEM((2, row_shards, PHASES, cols), jnp.bfloat16),
            pltpu.VMEM((CORES, taps, width, depth_rows), jnp.bfloat16),
            pltpu.VMEM((TAP_SIDE * stack, TAP_SIDE * depth_rows), jnp.bfloat16),
            pltpu.VMEM((2, (rows + 1) * depth_rows, rows_here * cols), jnp.bfloat16),
            pltpu.VMEM((2, 2, TAP_SIDE * stack, rows_here * cols), jnp.float32),
            pltpu.VMEM((row_shards, stack, cols), jnp.float32),
            pltpu.VMEM((row_shards, depths, lines, cols), jnp.int32),
            pltpu.VMEM((row_shards // CORES, frames, depths, lines, cols), jnp.int32),
            pltpu.SemaphoreType.REGULAR, dma((3,)), dma((2, 4)), dma((2, row_shards)), dma, dma, dma((row_shards, depths)),
            dma((row_shards // CORES, frames, depths)),
        ],
        compiler_params=pltpu.CompilerParams(collective_id=0, has_side_effects=True, vmem_limit_bytes=24 << 20),
    )(*[pltpu.with_memory_space_constraint(each, pltpu.HBM) for each in (volume.reshape(rows_here, merged), spread, region_map)])
    camera, residual = pl.pallas_call(
        hand_over,
        out_shape=[jax.ShapeDtypeStruct(image, jnp.float32)] * 2,
        in_specs=[vmem] * 3,
        out_specs=[vmem, vmem],
        compiler_params=pltpu.CompilerParams(vmem_limit_bytes=4 << 20),
    )(camera, measured.reshape(image), pixel_weight.reshape(image))
    return (camera.reshape(measured.shape), residual.reshape(measured.shape))


def solution(mesh):
    in_specs = (
        P("depth", "frame", "row", None),
        P("depth", "frame", None, "row"),
        P(),
        P("frame", "row", "depth"),
        P("frame", "row", "depth"),
    )
    out_specs = (P("frame", "row", "depth"), P("frame", "row", "depth"))
    sizes = (mesh.shape["frame"], mesh.shape["depth"], mesh.shape["row"])

    def body(volume, *rest):
        blocks_fit = rest[0].shape[1] % PHASES == 0
        stack = CORES * rest[0].shape[3]
        packs = sizes[1] == 4 and stack % 8 == 0 and stack // 8 % sizes[1] == 1
        pairs = volume.shape[2] == 2 and (volume.shape[3] // PHASES) == 128
        if sizes[0] == 2 and sizes[2] == 2 * CORES and volume.shape[1] == 1 and blocks_fit and packs and pairs:
            return fused_body(sizes, volume, *rest)
        return plain_body(volume, *rest)

    return jax.shard_map(body, mesh=mesh, in_specs=in_specs, out_specs=out_specs, check_vma=False)
```
